32 devices in a mesh: section: 4 (over z), head: 8 (over y, x, core).
Axes of the slice: x: 2, y: 2, z: 4, core: 2. Of those that a mesh axis runs over, the one named last changes fastest.
Arguments:
- prompt_states: bfloat16 [1, 128, 8192], P(None, 'head'), may hold values from -6 to 6
- norm_gain: float32 [4, 8192], P('section'), may hold values from 0.1 to 1.9
- query_weight: bfloat16 [4, 8192, 8192], P('section', None, 'head')
- key_weight: bfloat16 [4, 8192, 1024], P('section', None, 'head')
- value_weight: bfloat16 [4, 8192, 1024], P('section', None, 'head'), may hold values from -0.0625 to 0.0625
- out_weight: bfloat16 [4, 8192, 8192], P('section', 'head'), may hold values from -1 to 1
- cache_keys: bfloat16 [4, 4096, 1024], P('section', None, 'head'), may hold values from -6 to 6
- cache_values: bfloat16 [4, 4096, 1024], P('section', None, 'head'), may hold values from -6 to 6
- block_lists: int32 [1, 8], replicated, may hold values from 0 to 32, as said below
Outputs:
- section_states: bfloat16 [4, 1, 128, 8192], P('section', None, 'head')
The draws below stay inside these ranges and needn't reach their ends.
Inputs may be any that keep to these rules, and one draw needn't show every extreme that they name: `block_lists`: row i lists 8 distinct key blocks; block 32 + i is among them and none is greater.
All inputs are finite; a program needn't handle non-finite values.
Results may differ from the reference program's by a relative error of at most 0.024.
Values may be sent and summed in bfloat16 or wider, within the bound.
No kernel may reach another device: no remote copies, remote signals or barrier semaphores. Data moves between devices by JAX's collectives and lax.ppermute only.
A program may use at most 128 MiB of HBM per device.

```python
import math
import jax
import jax.numpy as jnp
from jax import lax

D = 8192
HEADS = 64
KVH = 8
HD = 128
BLOCK = 128
WIN = 3
GLOB = 2
RAND = 3
SPAN = 128
SPANS = 1
PREFIX = 4096
LAYERS = 4
TOKENS = 128
QBLOCKS = 1
NB = 8
N_HEAD = 8


def shared_keys(key):
    return jax.random.normal(jax.random.fold_in(key, 7), (LAYERS, D, KVH * HD), jnp.float32)


def draw_key_weight(key, part):
    return (shared_keys(key) / math.sqrt(D)).astype(jnp.bfloat16)


def draw_query_weight(key, part):
    noise_draw = jax.random.normal(jax.random.fold_in(key, 11), (LAYERS, D, HEADS * HD), jnp.float32)
    weights = noise_draw
    return (weights / math.sqrt(D)).astype(jnp.bfloat16)


def draw_block_lists(key, part):
    own_block = PREFIX // BLOCK + jnp.arange(QBLOCKS, dtype=jnp.int32)
    kblocks = PREFIX // BLOCK + QBLOCKS
    window_blocks = own_block[:, None] - jnp.arange(WIN, dtype=jnp.int32)[None, :]
    global_blocks = jnp.broadcast_to(jnp.arange(GLOB, dtype=jnp.int32)[None, :], (QBLOCKS, GLOB))
    candidates = jnp.arange(kblocks, dtype=jnp.int32)
    usable = (candidates[None, :] >= GLOB) & (candidates[None, :] < (own_block - WIN + 1)[:, None])
    ranking = jax.random.randint(jax.random.fold_in(key, 17), (QBLOCKS, kblocks), 0, 1 << 20, jnp.int32) * kblocks + candidates[None, :]
    ranking = jnp.where(usable, ranking, -1)
    chosen_values, chosen = lax.top_k(ranking, RAND)
    return jnp.concatenate([window_blocks, global_blocks, chosen.astype(jnp.int32)], 1).astype(jnp.int32)


def levels(own_key, dims, shards, smallest, largest):
    def one(position, shards_of):
        heights = jax.random.uniform(jax.random.fold_in(jax.random.fold_in(own_key, 6), position), (shards_of,), jnp.float32, smallest / len(shards), largest / len(shards))
        return jnp.repeat(jnp.exp(heights), dims[position] // shards_of).reshape((-1,) + (1,) * (len(dims) - position - 1))

    loudness = one(*shards[0])
    for cut in shards[1:]:
        loudness = loudness * one(*cut)
    return loudness


def bell_draw(key, dims, width, reach, cuts=(), held_as=jnp.bfloat16):
    drawn = width * jax.random.normal(key, dims, jnp.float32)
    if cuts:
        drawn = drawn * levels(key, dims, cuts, -0.22, 0.18)
    return jnp.clip(drawn, -reach, reach).astype(held_as)


def setup_inputs(seed: int = 0) -> dict:
    key_of = jax.random.split(jax.random.key(seed), 10)
    return {
        "prompt_states": bell_draw(key_of[0], (SPANS, SPAN, D), 1.0, 6.0, ((1, 8),)),
        "norm_gain": jnp.clip(1.0 + 0.18 * jax.random.normal(key_of[1], (LAYERS, D), jnp.float32), 0.1, 1.9),
        "query_weight": draw_query_weight(jax.random.fold_in(key_of[9], 71), 0),
        "key_weight": draw_key_weight(jax.random.fold_in(key_of[9], 71), 0),
        "value_weight": bell_draw(key_of[4], (LAYERS, D, KVH * HD), D ** -0.5, 0.0625, ((0, 4), (2, 8))),
        "out_weight": bell_draw(key_of[5], (LAYERS, HEADS * HD, D), (HD // 4) ** -0.5, 1.0, ((0, 4), (1, 8))),
        "cache_keys": bell_draw(key_of[6], (LAYERS, PREFIX, KVH * HD), 1.0, 6.0, ((0, 4), (2, 8))),
        "cache_values": bell_draw(key_of[7], (LAYERS, PREFIX, KVH * HD), 1.0, 6.0, ((0, 4), (2, 8))),
        "block_lists": draw_block_lists(jax.random.fold_in(key_of[9], 71), 0),
    }


EPS = 1e-05
THETA = 500000.0

def rotary(values, cosine, sine_rows):
    half_dim = values.shape[-1] // 2
    first_half = values[..., :half_dim]
    second_half = values[..., half_dim:]
    return jnp.concatenate([first_half * cosine - second_half * sine_rows, second_half * cosine + first_half * sine_rows], -1)

def reference(prompt_states, norm_gain, query_weight, key_weight, value_weight, out_weight, cache_keys, cache_values, block_lists):
    residual = prompt_states.reshape(TOKENS, D)
    positions = (PREFIX + jnp.arange(TOKENS, dtype=jnp.int32)).astype(jnp.float32)
    inverse_freq = jnp.exp(-math.log(THETA) * jnp.arange(HD // 2, dtype=jnp.float32) * 2.0 / HD)
    angles = positions[:, None] * inverse_freq[None, :]
    cosine = jnp.cos(angles)[:, None, :]
    sine_rows = jnp.sin(angles)[:, None, :]
    kblocks = PREFIX // BLOCK + QBLOCKS
    group_heads = HEADS // KVH
    scale = 1.0 / math.sqrt(HD)
    key_positions = (block_lists[:, :, None] * BLOCK + jnp.arange(BLOCK, dtype=jnp.int32)[None, None, :]).reshape(QBLOCKS, NB * BLOCK)
    query_positions = (PREFIX + jnp.arange(TOKENS, dtype=jnp.int32)).reshape(QBLOCKS, BLOCK)
    allowed = key_positions[:, None, None, None, :] <= query_positions[:, None, None, :, None]
    group_cols = HEADS * HD // N_HEAD
    collected = []
    for layer_index in range(LAYERS):
        widened = residual.astype(jnp.float32)
        normed = (widened * lax.rsqrt(lax.optimization_barrier(jnp.mean(widened * widened, -1, keepdims=True)) + EPS) * norm_gain[layer_index]).astype(jnp.bfloat16)
        queries = jnp.dot(normed, query_weight[layer_index], preferred_element_type=jnp.float32)
        queries = rotary(queries.reshape(TOKENS, HEADS, HD), cosine, sine_rows).astype(jnp.bfloat16)
        key_raw = jnp.dot(normed, key_weight[layer_index], preferred_element_type=jnp.float32).astype(jnp.bfloat16)
        key_raw = lax.optimization_barrier(key_raw)
        new_values = jnp.dot(normed, value_weight[layer_index], preferred_element_type=jnp.float32).astype(jnp.bfloat16)
        new_keys = rotary(key_raw.astype(jnp.float32).reshape(TOKENS, KVH, HD), cosine, sine_rows).astype(jnp.bfloat16)
        all_keys = jnp.concatenate([cache_keys[layer_index].reshape(PREFIX, KVH, HD), new_keys], 0)
        all_values = jnp.concatenate([cache_values[layer_index].reshape(PREFIX, KVH, HD), new_values.reshape(TOKENS, KVH, HD)], 0)
        key_blocks = all_keys.reshape(kblocks, BLOCK, KVH, HD)[block_lists].reshape(QBLOCKS, NB * BLOCK, KVH, HD).astype(jnp.float32)
        value_blocks = all_values.reshape(kblocks, BLOCK, KVH, HD)[block_lists].reshape(QBLOCKS, NB * BLOCK, KVH, HD).astype(jnp.float32)
        grouped = queries.reshape(QBLOCKS, BLOCK, KVH, group_heads, HD).astype(jnp.float32)
        scores = jnp.einsum('abkgd,ankd->akgbn', grouped, key_blocks) * scale
        scores = jnp.where(allowed, scores, -1e+30)
        row_peak = lax.optimization_barrier(jnp.max(scores, -1, keepdims=True))
        probabilities = jnp.exp(scores - row_peak)
        totals = lax.optimization_barrier(jnp.sum(probabilities, -1))
        weights = lax.optimization_barrier(probabilities.astype(jnp.bfloat16)).astype(jnp.float32)
        mixed = jnp.einsum('akgbn,ankd->abkgd', weights, value_blocks)
        mixed = mixed / jnp.transpose(totals, (0, 3, 1, 2))[..., None]
        attended = mixed.reshape(TOKENS, HEADS * HD).astype(jnp.bfloat16)
        summed = jnp.zeros((TOKENS, D), jnp.float32)
        for group in range(N_HEAD):
            partial_value = jnp.dot(attended[:, group * group_cols:(group + 1) * group_cols], out_weight[layer_index, group * group_cols:(group + 1) * group_cols], preferred_element_type=jnp.float32).astype(jnp.bfloat16)
            summed = summed + lax.optimization_barrier(partial_value).astype(jnp.float32)
        residual = (widened + summed).astype(jnp.bfloat16)
        collected.append(residual.reshape(SPANS, SPAN, D))
    return jnp.stack(collected)
```

```python
import functools
import math

import jax
import jax.numpy as jnp
from jax import lax
from jax.experimental import pallas as pl
from jax.experimental.pallas import tpu as pltpu
from jax.sharding import PartitionSpec as P

HD = 128
BLOCK = 128
EPS = 1e-05
THETA = 500000.0
CHUNKS = 8
MASKED = -1e30


def exchange(value, distance):
    count = lax.axis_size("head")
    return lax.ppermute(value, "head", [(i, i ^ distance) for i in range(count)])


def forward(value, section):
    return lax.ppermute(value, "section", [(section - 1, section)])


def join_columns(part, group_bits, head_index):
    for bit in range(group_bits):
        other = exchange(part, 1 << bit)
        is_lower = head_index >> bit & 1 == 0
        part = jnp.where(
            is_lower, jnp.concatenate([part, other], -1), jnp.concatenate([other, part], -1)
        )
    return part


def layer_kernel(
    piece_count,
    cached_blocks,
    lists_ref,
    *refs,
):
    pieces = refs[:piece_count]
    (wq_hbm, wk_hbm, wv_hbm, wo_hbm, keys_hbm, values_hbm) = refs[piece_count : piece_count + 6]
    cos_ref, sin_ref, row_ref, col_ref = refs[piece_count + 6 : piece_count + 10]
    outs = refs[piece_count + 10 : 2 * piece_count + 10]
    (x_s, wq_s, wk_s, wv_s, wo_s, k_s, v_s, q_s, kv_s, att_s, sem_q, sem_kv, sem_o, sem_c) = refs[
        2 * piece_count + 10 :
    ]
    tokens = x_s.shape[1]
    depth = x_s.shape[2]
    rows = pieces[0].shape[0]
    query_cols = wq_s.shape[2]
    out_cols = wo_s.shape[2]
    query_heads = query_cols // HD
    listed = k_s.shape[0] // BLOCK

    def query_copy(k):
        return pltpu.make_async_copy(
            wq_hbm.at[0, pl.ds(k * depth, depth), :], wq_s.at[k], sem_q.at[k]
        )

    def key_copy():
        return pltpu.make_async_copy(wk_hbm.at[0], wk_s, sem_kv.at[0])

    def value_copy():
        return pltpu.make_async_copy(wv_hbm.at[0], wv_s, sem_kv.at[1])

    def out_copy(n):
        return pltpu.make_async_copy(
            wo_hbm.at[0, :, pl.ds(n * out_cols, out_cols)], wo_s.at[n], sem_o.at[n]
        )

    cache_copies = []
    passed = lists_ref[0, 0] == cached_blocks
    for j in range(listed - 1):
        if j:
            passed = passed | (lists_ref[0, j] == cached_blocks)
        block = jnp.where(passed, lists_ref[0, j + 1], lists_ref[0, j])
        block = jnp.clip(block, 0, cached_blocks - 1)
        start = pl.multiple_of(block * BLOCK, BLOCK)
        for which, (source, target) in enumerate(((keys_hbm, k_s), (values_hbm, v_s))):
            cache_copies.append(
                pltpu.make_async_copy(
                    source.at[0, pl.ds(start, BLOCK), :],
                    target.at[pl.ds(j * BLOCK, BLOCK), :],
                    sem_c.at[which, j],
                )
            )

    key_copy().start()
    value_copy().start()
    for k in range(CHUNKS):
        query_copy(k).start()
    for copy in cache_copies:
        copy.start()
    for n in range(CHUNKS):
        out_copy(n).start()

    for k in range(CHUNKS):
        for p, piece in enumerate(pieces):
            x_s[k, p * rows : (p + 1) * rows, :] = piece[:, k * depth : (k + 1) * depth]

    key_copy().wait()
    value_copy().wait()

    def project(k, carry):
        query_copy(k).wait()
        x = x_s[k]
        start = pl.multiple_of(k * depth, depth)
        q_new = jnp.dot(x, wq_s[k], preferred_element_type=jnp.float32)
        k_new = jnp.dot(x, wk_s[pl.ds(start, depth), :], preferred_element_type=jnp.float32)
        v_new = jnp.dot(x, wv_s[pl.ds(start, depth), :], preferred_element_type=jnp.float32)

        @pl.when(k == 0)
        def _():
            q_s[...] = q_new
            kv_s[0] = k_new
            kv_s[1] = v_new

        @pl.when(k != 0)
        def _():
            q_s[...] += q_new
            kv_s[0] += k_new
            kv_s[1] += v_new

        return carry

    lax.fori_loop(0, CHUNKS, project, 0)

    cosine, sine = cos_ref[...], sin_ref[...]

    def rotated(value):
        return (value * cosine + pltpu.roll(value, HD // 2, 1) * sine).astype(jnp.bfloat16)

    k_s[(listed - 1) * BLOCK :, :] = rotated(kv_s[0].astype(jnp.bfloat16).astype(jnp.float32))
    v_s[(listed - 1) * BLOCK :, :] = kv_s[1].astype(jnp.bfloat16)
    for copy in cache_copies:
        copy.wait()
    keys, values = k_s[...], v_s[...]
    allowed = col_ref[...] <= row_ref[...]
    factor = math.log2(math.e) / math.sqrt(HD)
    for head in range(query_heads):
        columns = slice(head * HD, (head + 1) * HD)
        query = rotated(q_s[:, columns])
        scores = lax.dot_general(
            query, keys, (((1,), (1,)), ((), ())), preferred_element_type=jnp.float32
        )
        scores = jnp.concatenate(
            [
                scores[:, : (listed - 1) * BLOCK],
                jnp.where(allowed, scores[:, (listed - 1) * BLOCK :], MASKED),
            ],
            1,
        )
        peak = jnp.max(scores, -1, keepdims=True)
        probabilities = jnp.exp2((scores - peak) * factor)
        totals = jnp.sum(probabilities, -1, keepdims=True)
        mixed = jnp.dot(
            probabilities.astype(jnp.bfloat16), values, preferred_element_type=jnp.float32
        )
        att_s[:, columns] = (mixed / totals).astype(jnp.bfloat16)

    def give(n, carry):
        out_copy(n).wait()
        result = jnp.dot(att_s[...], wo_s[n], preferred_element_type=jnp.float32)
        result = result.astype(jnp.bfloat16)
        columns = pl.ds(pl.multiple_of(n * out_cols, out_cols), out_cols)
        for p, out in enumerate(outs):
            out[:, columns] = result[p * rows : (p + 1) * rows]
        return carry

    lax.fori_loop(0, CHUNKS, give, 0)


def layer(pieces, weights, cache, lists, tables):
    query_weight, key_weight, value_weight, out_weight = weights
    width = query_weight.shape[1]
    query_cols = query_weight.shape[2]
    listed = lists.shape[1]
    rows = pieces[0].shape[0]
    tokens = rows * len(pieces)
    depth, out_cols = width // CHUNKS, out_weight.shape[2] // CHUNKS
    vmem = pl.BlockSpec(memory_space=pltpu.VMEM)
    anywhere = pl.BlockSpec(memory_space=pl.ANY)
    size = 2 * (width * (query_cols + 2 * HD) + query_cols * out_weight.shape[2])
    return pl.pallas_call(
        functools.partial(layer_kernel, len(pieces), cache[0].shape[1] // BLOCK),
        out_shape=[jax.ShapeDtypeStruct((rows, out_weight.shape[2]), jnp.bfloat16)] * len(pieces),
        in_specs=[pl.BlockSpec(memory_space=pltpu.SMEM)]
        + [vmem] * len(pieces)
        + [anywhere] * 6
        + [vmem] * 4,
        out_specs=[vmem] * len(pieces),
        scratch_shapes=[
            pltpu.VMEM((CHUNKS, tokens, depth), jnp.bfloat16),
            pltpu.VMEM((CHUNKS, depth, query_cols), jnp.bfloat16),
            pltpu.VMEM((width, HD), jnp.bfloat16),
            pltpu.VMEM((width, HD), jnp.bfloat16),
            pltpu.VMEM((CHUNKS, query_cols, out_cols), jnp.bfloat16),
            pltpu.VMEM((listed * BLOCK, HD), jnp.bfloat16),
            pltpu.VMEM((listed * BLOCK, HD), jnp.bfloat16),
            pltpu.VMEM((tokens, query_cols), jnp.float32),
            pltpu.VMEM((2, tokens, HD), jnp.float32),
            pltpu.VMEM((tokens, query_cols), jnp.bfloat16),
            pltpu.SemaphoreType.DMA((CHUNKS,)),
            pltpu.SemaphoreType.DMA((2,)),
            pltpu.SemaphoreType.DMA((CHUNKS,)),
            pltpu.SemaphoreType.DMA((2, listed - 1)),
        ],
        compiler_params=pltpu.CompilerParams(vmem_limit_bytes=52 << 20),
        cost_estimate=pl.CostEstimate(
            flops=tokens * size, bytes_accessed=size, transcendentals=tokens * listed * BLOCK * 8
        ),
        name="attention_sublayer",
    )(lists, *pieces, *weights, *cache, *tables)


def gather_rows(own):
    count = lax.axis_size("head")
    pieces = [own if not j else exchange(own, j) for j in range(0, count, 2)]
    return [p for piece in pieces for p in (piece, exchange(piece, 1))]


def scatter_rows(partials):
    count = lax.axis_size("head")
    terms = []
    for j in reversed(range(0, count, 2)):
        both = partials[j].astype(jnp.float32) + exchange(partials[j + 1], 1).astype(jnp.float32)
        both = both.astype(jnp.bfloat16)
        terms.append(exchange(both, j) if j else both)
    return terms


def on_device(
    prompt_states,
    norm_gain,
    query_weight,
    key_weight,
    value_weight,
    out_weight,
    cache_keys,
    cache_values,
    block_lists,
):
    sections = lax.axis_size("section")
    heads = lax.axis_size("head")
    section_index = lax.axis_index("section")
    head_index = lax.axis_index("head")
    rows = prompt_states.shape[1]
    tokens = rows * heads
    prefix = cache_keys.shape[1]
    group_bits = (HD // key_weight.shape[2]).bit_length() - 1
    weights = (
        query_weight,
        join_columns(key_weight, group_bits, head_index),
        join_columns(value_weight, group_bits, head_index),
        out_weight,
    )
    cache = (
        join_columns(cache_keys, group_bits, head_index),
        join_columns(cache_values, group_bits, head_index),
    )
    gain_row = norm_gain[0]

    whole_tiles = rows % 16 == 0
    block_of = jnp.arange(heads, dtype=jnp.int32) ^ head_index
    positions = (
        prefix + block_of[:, None] * rows + jnp.arange(rows, dtype=jnp.int32)[None, :]
    ).reshape(tokens)
    inverse_freq = jnp.exp(-math.log(THETA) * jnp.arange(HD // 2, dtype=jnp.float32) * 2.0 / HD)
    angles = positions.astype(jnp.float32)[:, None] * inverse_freq[None, :]
    cosine, sine = jnp.cos(angles), jnp.sin(angles)
    tables = (
        jnp.concatenate([cosine, cosine], 1),
        jnp.concatenate([-sine, sine], 1),
        positions[:, None],
        positions[None, :],
    )

    states = prompt_states[0]
    output = jnp.zeros_like(states)
    for step in range(sections):
        if step:
            states = forward(states, step)
        widened = states.astype(jnp.float32)
        normed = (
            widened * lax.rsqrt(jnp.mean(widened * widened, -1, keepdims=True) + EPS) * gain_row
        ).astype(jnp.bfloat16)
        pieces = gather_rows(normed)
        if not whole_tiles:
            pieces = [jnp.concatenate(pieces, 0)]
        partials = layer(pieces, weights, cache, block_lists, tables)
        if not whole_tiles:
            partials = jnp.split(partials[0], heads, 0)
        summed = sum(term.astype(jnp.float32) for term in scatter_rows(partials))
        states = (widened + summed).astype(jnp.bfloat16)
        output = jnp.where(section_index == step, states, output)
    return output[None, None]


def solution(mesh):
    return jax.shard_map(
        on_device,
        mesh=mesh,
        in_specs=(
            P(None, "head", None),
            P("section", None),
            P("section", None, "head"),
            P("section", None, "head"),
            P("section", None, "head"),
            P("section", "head", None),
            P("section", None, "head"),
            P("section", None, "head"),
            P(),
        ),
        out_specs=P("section", None, "head", None),
        check_vma=False,
    )
```

```python
import functools
import math

import jax
import jax.numpy as jnp
from jax import lax
from jax.experimental import pallas as pl
from jax.experimental.pallas import tpu as pltpu
from jax.sharding import PartitionSpec as P

HD = 128
BLOCK = 128
EPS = 1e-05
THETA = 500000.0
CHUNKS = 8
HALVES = 2
MASKED = -1e30


def exchange(value, distance):
    count = lax.axis_size("head")
    return lax.ppermute(value, "head", [(i, i ^ distance) for i in range(count)])


def forward(value, section):
    count = lax.axis_size("section")
    there = {section - 1: section, section: section - 1}
    return lax.ppermute(value, "section", [(i, there.get(i, i)) for i in range(count)])


def join_columns(part, group_bits, head_index):
    for bit in range(group_bits):
        other = exchange(part, 1 << bit)
        is_lower = head_index >> bit & 1 == 0
        part = jnp.where(
            is_lower, jnp.concatenate([part, other], -1), jnp.concatenate([other, part], -1)
        )
    return part


def loader_kernel(cuts, *refs):
    targets, sems = refs[len(cuts) : -1], refs[-1]
    sources = []
    for ref, (axis, count) in zip(refs, cuts):
        size = ref.shape[axis] // count
        for k in range(count):
            part = pl.ds(k * size, size)
            sources.append(ref.at[0, part, :] if axis == 1 else ref.at[0, :, part])
    copies = [
        pltpu.make_async_copy(source, target, sems.at[i])
        for i, (source, target) in enumerate(zip(sources, targets))
    ]
    for copy in copies:
        copy.start()
    for copy in copies:
        copy.wait()


def load(weights, cuts):
    shapes = []
    for weight, (axis, count) in zip(weights, cuts):
        shape = list(weight.shape)
        shape[axis] //= count
        shapes += [tuple(shape[1:])] * count
    size = sum(w.size * w.dtype.itemsize for w in weights)
    return pl.pallas_call(
        functools.partial(loader_kernel, cuts),
        out_shape=[pltpu.VMEM(shape, jnp.bfloat16) for shape in shapes],
        in_specs=[pl.BlockSpec(memory_space=pltpu.HBM)] * len(weights),
        out_specs=[pl.BlockSpec(memory_space=pltpu.VMEM)] * len(shapes),
        scratch_shapes=[pltpu.SemaphoreType.DMA((len(shapes),))],
        compiler_params=pltpu.CompilerParams(vmem_limit_bytes=1 << 20),
        cost_estimate=pl.CostEstimate(flops=0, bytes_accessed=2 * size, transcendentals=0),
        name="load_weights",
    )(*[pltpu.with_memory_space_constraint(w, pltpu.HBM) for w in weights])


def layer_kernel(piece_count, cached_blocks, device_rows, targets, lists_ref, place_ref, *refs):
    pieces = refs[:piece_count]
    refs = refs[piece_count:]
    wq_refs, wk_ref, wv_ref = refs[:CHUNKS], refs[CHUNKS], refs[CHUNKS + 1]
    wo_refs = refs[CHUNKS + 2 : 2 * CHUNKS + 2]
    refs = refs[2 * CHUNKS + 2 :]
    keys_hbm, values_hbm, gain_ref, cos_ref, sin_ref = refs[:5]
    outs = refs[5:-4]
    k_s, v_s, att_s, sem_c = refs[-4:]
    row_blocks = piece_count // HALVES
    rows, half = pieces[0].shape
    depth, query_cols = wq_refs[0].shape
    width = depth * CHUNKS
    out_cols = wo_refs[0].shape[1]
    out_half = out_cols * CHUNKS // HALVES
    query_heads = query_cols // HD
    listed = k_s.shape[0] // BLOCK

    cache_copies = []
    passed = lists_ref[0, 0] == cached_blocks
    for j in range(listed - 1):
        if j:
            passed = passed | (lists_ref[0, j] == cached_blocks)
        block = jnp.where(passed, lists_ref[0, j + 1], lists_ref[0, j])
        block = jnp.clip(block, 0, cached_blocks - 1)
        start = pl.multiple_of(block * BLOCK, BLOCK)
        for which, (source, target) in enumerate(((keys_hbm, k_s), (values_hbm, v_s))):
            cache_copies.append(
                pltpu.make_async_copy(
                    source.at[0, pl.ds(start, BLOCK), :],
                    target.at[pl.ds(j * BLOCK, BLOCK), :],
                    sem_c.at[which, j],
                )
            )
    for copy in cache_copies:
        copy.start()

    queries = new_keys = new_values = squares = 0.0
    for k in range(CHUNKS):
        part = slice(k * depth, (k + 1) * depth)
        which, inner = k * depth // half, k * depth % half
        x = jnp.concatenate(
            [
                pieces[which * row_blocks + p][:, inner : inner + depth]
                for p in range(row_blocks)
            ],
            0,
        ).astype(jnp.float32)
        squares += jnp.sum(x * x, -1, keepdims=True)
        x = (x * gain_ref[:, part]).astype(jnp.bfloat16)
        queries += jnp.dot(x, wq_refs[k][...], preferred_element_type=jnp.float32)
        new_keys += jnp.dot(x, wk_ref[part, :], preferred_element_type=jnp.float32)
        new_values += jnp.dot(x, wv_ref[part, :], preferred_element_type=jnp.float32)

    norm = lax.rsqrt(squares / width + EPS)
    cosine, sine = cos_ref[...], sin_ref[...]

    def rotated(value):
        return (value * cosine + pltpu.roll(value, HD // 2, 1) * sine).astype(jnp.bfloat16)

    new_keys = (new_keys * norm).astype(jnp.bfloat16).astype(jnp.float32)
    k_s[(listed - 1) * BLOCK :, :] = rotated(new_keys)
    v_s[(listed - 1) * BLOCK :, :] = (new_values * norm).astype(jnp.bfloat16)
    for copy in cache_copies:
        copy.wait()
    keys, values = k_s[...], v_s[...]

    def token(axis):
        index = lax.broadcasted_iota(jnp.int32, (BLOCK, BLOCK), axis)
        return (index // device_rows ^ place_ref[1]) * device_rows + index % device_rows

    allowed = token(1) <= token(0)
    factor = math.log2(math.e) / math.sqrt(HD)
    for head in range(query_heads):
        columns = slice(head * HD, (head + 1) * HD)
        query = rotated(queries[:, columns] * norm)
        scores = lax.dot_general(
            query, keys, (((1,), (1,)), ((), ())), preferred_element_type=jnp.float32
        )
        scores = jnp.concatenate(
            [
                scores[:, : (listed - 1) * BLOCK],
                jnp.where(allowed, scores[:, (listed - 1) * BLOCK :], MASKED),
            ],
            1,
        )
        peak = jnp.max(scores, -1, keepdims=True)
        probabilities = jnp.exp2((scores - peak) * factor)
        totals = jnp.sum(probabilities, -1, keepdims=True)
        mixed = jnp.dot(
            probabilities.astype(jnp.bfloat16), values, preferred_element_type=jnp.float32
        )
        att_s[:, columns] = (mixed / totals).astype(jnp.bfloat16)

    attended = att_s[...]
    for n in range(CHUNKS):
        which, inner = n * out_cols // out_half, n * out_cols % out_half
        result = jnp.dot(attended, wo_refs[n][...], preferred_element_type=jnp.float32)
        result = result.astype(jnp.bfloat16)
        for p, (out, row) in enumerate(targets[which]):
            outs[out][row : row + rows, inner : inner + out_cols] = result[
                p * rows : (p + 1) * rows
            ]


def layer(pieces, targets, out_rows, device_rows, weights, cache, lists, place, tables):
    depth, query_cols = weights[0].shape
    width = depth * CHUNKS
    out_half = weights[-1].shape[1] * CHUNKS // HALVES
    listed = lists.shape[1]
    rows = pieces[0].shape[0]
    tokens = rows * len(pieces) // HALVES
    vmem = pl.BlockSpec(memory_space=pltpu.VMEM)
    hbm = pl.BlockSpec(memory_space=pltpu.HBM)
    size = 2 * (width * (query_cols + 2 * HD) + query_cols * out_half * HALVES)
    return pl.pallas_call(
        functools.partial(
            layer_kernel, len(pieces), cache[0].shape[1] // BLOCK, device_rows, targets
        ),
        out_shape=[pltpu.VMEM((r, out_half), jnp.bfloat16) for r in out_rows],
        in_specs=[pl.BlockSpec(memory_space=pltpu.SMEM)] * 2
        + [vmem] * (len(pieces) + len(weights))
        + [hbm] * 2
        + [vmem] * 3,
        out_specs=[vmem] * len(out_rows),
        scratch_shapes=[
            pltpu.VMEM((listed * BLOCK, HD), jnp.bfloat16),
            pltpu.VMEM((listed * BLOCK, HD), jnp.bfloat16),
            pltpu.VMEM((tokens, query_cols), jnp.bfloat16),
            pltpu.SemaphoreType.DMA((2, listed - 1)),
        ],
        compiler_params=pltpu.CompilerParams(vmem_limit_bytes=10 << 20),
        cost_estimate=pl.CostEstimate(
            flops=tokens * size, bytes_accessed=size, transcendentals=tokens * listed * BLOCK * 8
        ),
        name="attention_sublayer",
    )(
        lists,
        place,
        *pieces,
        *weights,
        *[pltpu.with_memory_space_constraint(c, pltpu.HBM) for c in cache],
        *tables,
    )


def named(body, *args):
    bound = functools.partial(body, *args)
    bound.__name__ = body.__name__
    return bound


def chip_bits():
    return [1 << b for b in range(1, (lax.axis_size("head") - 1).bit_length())]


def small_call(body, shapes, *args):
    vmem = pl.BlockSpec(memory_space=pltpu.VMEM)
    size = sum(a.size * a.dtype.itemsize for a in args)
    return pl.pallas_call(
        body,
        out_shape=[pltpu.VMEM(shape, dtype) for shape, dtype in shapes],
        in_specs=[vmem if a.ndim > 1 else pl.BlockSpec(memory_space=pltpu.SMEM) for a in args],
        out_specs=[vmem] * len(shapes),
        compiler_params=pltpu.CompilerParams(vmem_limit_bytes=1 << 20),
        cost_estimate=pl.CostEstimate(flops=size, bytes_accessed=2 * size, transcendentals=0),
        name=body.__name__,
    )(*args)


def split_sum(own_ref, other_ref, kept_ref, sent_ref):
    cut = kept_ref.shape[0]
    kept_ref[...] = own_ref[:cut].astype(jnp.float32) + other_ref[:cut].astype(jnp.float32)
    sent_ref[...] = (
        own_ref[cut:].astype(jnp.float32) + other_ref[cut:].astype(jnp.float32)
    ).astype(sent_ref.dtype)


def last_sum(count, step, place_ref, *refs):
    states, kept, others = refs[:count], refs[count : 2 * count], refs[2 * count : 3 * count]
    earlier, outs = refs[3 * count : -2 * count], refs[-2 * count :]
    for i in range(count):
        new = states[i][...].astype(jnp.float32) + kept[i][...] + others[i][...].astype(jnp.float32)
        new = new.astype(jnp.bfloat16)
        outs[i][...] = new
        if earlier:
            new = jnp.where(place_ref[0] == step, new, earlier[i][...])
        outs[count + i][...] = new


def gather(states, orders, loads=()):
    halves = [{0: s} for s in states]
    loaded = []
    for phase in range(len(orders[0])):
        received = [
            {j ^ order[phase]: exchange(v, order[phase]) for j, v in blocks.items()}
            for blocks, order in zip(halves, orders)
        ]
        if phase < len(loads):
            received, weights = lax.optimization_barrier((received, loads[phase]))
            loaded += weights
        halves = [blocks | more for blocks, more in zip(halves, received)]
    for weights in loads[len(orders[0]) :]:
        loaded += weights
    halves = [blocks | {j ^ 1: exchange(v, 1) for j, v in blocks.items()} for blocks in halves]
    return [[blocks[j] for j in sorted(blocks)] for blocks in halves], loaded


def scatter_order(order, count):
    return sorted(range(0, count, 2), key=lambda j: [j & d for d in order])


def scatter_half(even, odd, order):
    kept, sent, other = even, None, exchange(odd, 1)
    for distance in order:
        rows, columns = kept.shape
        shape = (rows // 2, columns)
        kept, sent = small_call(
            split_sum, [(shape, jnp.float32), (shape, jnp.bfloat16)], kept, other
        )
        other = exchange(sent, distance)
    return kept, other


def on_device(
    prompt_states,
    norm_gain,
    query_weight,
    key_weight,
    value_weight,
    out_weight,
    cache_keys,
    cache_values,
    block_lists,
):
    sections = lax.axis_size("section")
    heads = lax.axis_size("head")
    section_index = lax.axis_index("section")
    head_index = lax.axis_index("head")
    rows, width = prompt_states.shape[1:]
    half = width // HALVES
    tokens = rows * heads
    prefix = cache_keys.shape[1]
    group_bits = (HD // key_weight.shape[2]).bit_length() - 1
    key_weight = join_columns(key_weight, group_bits, head_index)
    value_weight = join_columns(value_weight, group_bits, head_index)
    cache = (
        join_columns(cache_keys, group_bits, head_index),
        join_columns(cache_values, group_bits, head_index),
    )

    whole_tiles = rows % 16 == 0
    block_of = jnp.arange(heads, dtype=jnp.int32) ^ head_index
    positions = (
        prefix + block_of[:, None] * rows + jnp.arange(rows, dtype=jnp.int32)[None, :]
    ).reshape(tokens)
    inverse_freq = jnp.exp(-math.log(THETA) * jnp.arange(HD // 2, dtype=jnp.float32) * 2.0 / HD)
    angles = positions.astype(jnp.float32)[:, None] * inverse_freq[None, :]
    cosine, sine = jnp.cos(angles), jnp.sin(angles)
    tables = (
        norm_gain,
        jnp.concatenate([cosine, cosine], 1),
        jnp.concatenate([-sine, sine], 1),
    )
    place = jnp.stack([section_index, head_index]).astype(jnp.int32)
    projections = (query_weight, key_weight, value_weight)
    place, tables, projections, out_weight = lax.optimization_barrier(
        (place, tables, projections, out_weight)
    )

    orders = (chip_bits(), chip_bits()[::-1])
    if whole_tiles:
        targets = []
        for i, order in enumerate(orders):
            spots = {}
            for row, j in enumerate(scatter_order(order, heads)):
                spots |= {j: (2 * i, row * rows), j + 1: (2 * i + 1, row * rows)}
            targets.append(tuple(spots[j] for j in range(heads)))
        out_rows = [tokens // 2] * 2 * HALVES
    else:
        targets = [((i, 0),) for i in range(HALVES)]
        out_rows = [tokens] * HALVES

    loads = [
        load(projections, ((1, CHUNKS), (1, 1), (1, 1))),
        load((out_weight,), ((2, CHUNKS),)),
    ]
    states = [prompt_states[0, :, i * half : (i + 1) * half] for i in range(HALVES)]
    output, weights = [], None
    for step in range(sections):
        if step:
            states = [forward(s, step) for s in states]
        pieces, loaded = gather(states, orders, () if step else loads)
        weights = loaded or weights
        if not whole_tiles:
            pieces = [[jnp.concatenate(p, 0)] for p in pieces]
        partials = layer(
            sum(pieces, []), targets, out_rows, rows, weights, cache, block_lists, place, tables
        )
        if not whole_tiles:
            blocks = [jnp.split(p, heads, 0) for p in partials]
            partials = [
                jnp.concatenate([b[j + odd] for j in scatter_order(order, heads)], 0)
                for b, order in zip(blocks, orders)
                for odd in range(2)
            ]
        sums = [
            scatter_half(partials[2 * i], partials[2 * i + 1], order)
            for i, order in enumerate(orders)
        ]
        kept, others = zip(*sums)
        made = small_call(
            named(last_sum, HALVES, step),
            [((rows, half), jnp.bfloat16)] * 2 * HALVES,
            place,
            *states,
            *kept,
            *others,
            *output,
        )
        states, output = made[:HALVES], made[HALVES:]
    return jnp.concatenate(output, 1)[None, None]


def solution(mesh):
    return jax.shard_map(
        on_device,
        mesh=mesh,
        in_specs=(
            P(None, "head", None),
            P("section", None),
            P("section", None, "head"),
            P("section", None, "head"),
            P("section", None, "head"),
            P("section", "head", None),
            P("section", None, "head"),
            P("section", None, "head"),
            P(),
        ),
        out_specs=P("section", None, "head", None),
        check_vma=False,
    )
```

```python
import functools
import math

import jax
import jax.numpy as jnp
from jax import lax
from jax.experimental import pallas as pl
from jax.experimental.pallas import tpu as pltpu
from jax.sharding import PartitionSpec as P

HD = 128
BLOCK = 128
EPS = 1e-05
THETA = 500000.0
CHUNKS = 8
HALVES = 2
MASKED = -1e30


def exchange(value, distance):
    count = lax.axis_size("head")
    return lax.ppermute(value, "head", [(i, i ^ distance) for i in range(count)])


def forward(value, section):
    return lax.ppermute(value, "section", [(section - 1, section)])


def join_columns(part, group_bits, head_index):
    for bit in range(group_bits):
        other = exchange(part, 1 << bit)
        is_lower = head_index >> bit & 1 == 0
        part = jnp.where(
            is_lower, jnp.concatenate([part, other], -1), jnp.concatenate([other, part], -1)
        )
    return part


def loader_kernel(cuts, *refs):
    targets, sems = refs[len(cuts) : -1], refs[-1]
    sources = []
    for ref, (axis, count, first, last) in zip(refs, cuts):
        size = ref.shape[axis] // count
        for k in range(first, last):
            part = pl.ds(k * size, size)
            sources.append(ref.at[0, part, :] if axis == 1 else ref.at[0, :, part])
    copies = [
        pltpu.make_async_copy(source, target, sems.at[i])
        for i, (source, target) in enumerate(zip(sources, targets))
    ]
    for copy in copies:
        copy.start()
    for copy in copies:
        copy.wait()


def load(weights, cuts):
    shapes = []
    for weight, (axis, count, first, last) in zip(weights, cuts):
        shape = list(weight.shape)
        shape[axis] //= count
        shapes += [tuple(shape[1:])] * (last - first)
    size = sum(2 * math.prod(shape) for shape in shapes)
    return pl.pallas_call(
        functools.partial(loader_kernel, cuts),
        out_shape=[pltpu.VMEM(shape, jnp.bfloat16) for shape in shapes],
        in_specs=[pl.BlockSpec(memory_space=pltpu.HBM)] * len(weights),
        out_specs=[pl.BlockSpec(memory_space=pltpu.VMEM)] * len(shapes),
        scratch_shapes=[pltpu.SemaphoreType.DMA((len(shapes),))],
        compiler_params=pltpu.CompilerParams(vmem_limit_bytes=1 << 20),
        cost_estimate=pl.CostEstimate(flops=0, bytes_accessed=2 * size, transcendentals=0),
        name="load_weights",
    )(*[pltpu.with_memory_space_constraint(w, pltpu.HBM) for w in weights])


def layer_kernel(piece_count, cached_blocks, device_rows, targets, lists_ref, place_ref, *refs):
    pieces = refs[:piece_count]
    refs = refs[piece_count:]
    wq_refs, wk_ref, wv_ref = refs[:CHUNKS], refs[CHUNKS], refs[CHUNKS + 1]
    loads_out = len(refs[CHUNKS + 2].shape) == 3
    out_count = 1 if loads_out else CHUNKS
    wo_refs = refs[CHUNKS + 2 : CHUNKS + 2 + out_count]
    refs = refs[CHUNKS + 2 + out_count :]
    keys_hbm, values_hbm, gain_ref, cos_ref, sin_ref = refs[:5]
    outs = refs[5:-5]
    k_s, v_s, att_s, sem_c, sem_o = refs[-5:]
    out_copies = []
    if loads_out:
        source, outs, wo_refs = wo_refs[0], outs[:-CHUNKS], outs[-CHUNKS:]
        size = wo_refs[0].shape[1]
        for n, target in enumerate(wo_refs):
            part = source.at[0, :, pl.ds(n * size, size)]
            out_copies.append(pltpu.make_async_copy(part, target, sem_o.at[n]))
    row_blocks = piece_count // HALVES
    rows, half = pieces[0].shape
    depth, query_cols = wq_refs[0].shape
    width = depth * CHUNKS
    out_cols = wo_refs[0].shape[1]
    out_half = out_cols * CHUNKS // HALVES
    query_heads = query_cols // HD
    listed = k_s.shape[0] // BLOCK

    cache_copies = []
    passed = lists_ref[0, 0] == cached_blocks
    for j in range(listed - 1):
        if j:
            passed = passed | (lists_ref[0, j] == cached_blocks)
        block = jnp.where(passed, lists_ref[0, j + 1], lists_ref[0, j])
        block = jnp.clip(block, 0, cached_blocks - 1)
        start = pl.multiple_of(block * BLOCK, BLOCK)
        for which, (source, target) in enumerate(((keys_hbm, k_s), (values_hbm, v_s))):
            cache_copies.append(
                pltpu.make_async_copy(
                    source.at[0, pl.ds(start, BLOCK), :],
                    target.at[pl.ds(j * BLOCK, BLOCK), :],
                    sem_c.at[which, j],
                )
            )
    for copy in cache_copies + out_copies:
        copy.start()

    queries = new_keys = new_values = squares = 0.0
    for k in range(CHUNKS):
        part = slice(k * depth, (k + 1) * depth)
        which, inner = k * depth // half, k * depth % half
        x = jnp.concatenate(
            [
                pieces[which * row_blocks + p][:, inner : inner + depth]
                for p in range(row_blocks)
            ],
            0,
        ).astype(jnp.float32)
        squares += jnp.sum(x * x, -1, keepdims=True)
        x = (x * gain_ref[:, part]).astype(jnp.bfloat16)
        queries += jnp.dot(x, wq_refs[k][...], preferred_element_type=jnp.float32)
        new_keys += jnp.dot(x, wk_ref[part, :], preferred_element_type=jnp.float32)
        new_values += jnp.dot(x, wv_ref[part, :], preferred_element_type=jnp.float32)

    norm = lax.rsqrt(squares / width + EPS)
    cosine, sine = cos_ref[...], sin_ref[...]

    def rotated(value):
        return (value * cosine + pltpu.roll(value, HD // 2, 1) * sine).astype(jnp.bfloat16)

    new_keys = (new_keys * norm).astype(jnp.bfloat16).astype(jnp.float32)
    k_s[(listed - 1) * BLOCK :, :] = rotated(new_keys)
    v_s[(listed - 1) * BLOCK :, :] = (new_values * norm).astype(jnp.bfloat16)
    for copy in cache_copies:
        copy.wait()
    keys, values = k_s[...], v_s[...]

    def token(axis):
        index = lax.broadcasted_iota(jnp.int32, (BLOCK, BLOCK), axis)
        return (index // device_rows ^ place_ref[1]) * device_rows + index % device_rows

    allowed = token(1) <= token(0)
    factor = math.log2(math.e) / math.sqrt(HD)
    together = 2 if query_heads % 2 == 0 else 1
    allowed = jnp.concatenate([allowed] * together, 0)
    norms = jnp.concatenate([norm] * together, 0)
    cosine, sine = (jnp.concatenate([t] * together, 0) for t in (cosine, sine))
    for first in range(0, query_heads, together):
        heads = range(first, first + together)
        query = jnp.concatenate([queries[:, h * HD : (h + 1) * HD] for h in heads], 0)
        scores = lax.dot_general(
            rotated(query * norms),
            keys,
            (((1,), (1,)), ((), ())),
            preferred_element_type=jnp.float32,
        )
        scores = jnp.concatenate(
            [
                scores[:, : (listed - 1) * BLOCK],
                jnp.where(allowed, scores[:, (listed - 1) * BLOCK :], MASKED),
            ],
            1,
        )
        peak = jnp.max(scores, -1, keepdims=True)
        probabilities = jnp.exp2((scores - peak) * factor)
        totals = jnp.sum(probabilities, -1, keepdims=True)
        mixed = jnp.dot(
            probabilities.astype(jnp.bfloat16), values, preferred_element_type=jnp.float32
        )
        mixed = (mixed / totals).astype(jnp.bfloat16)
        for i, h in enumerate(heads):
            att_s[:, h * HD : (h + 1) * HD] = mixed[i * BLOCK : (i + 1) * BLOCK]

    attended = att_s[...]
    for n in range(CHUNKS):
        which, inner = n * out_cols // out_half, n * out_cols % out_half
        if loads_out:
            out_copies[n].wait()
        result = jnp.dot(attended, wo_refs[n][...], preferred_element_type=jnp.float32)
        result = result.astype(jnp.bfloat16)
        for p, (out, row) in enumerate(targets[which]):
            outs[out][row : row + rows, inner : inner + out_cols] = result[
                p * rows : (p + 1) * rows
            ]


def layer(pieces, targets, out_rows, device_rows, weights, cache, lists, place, tables):
    depth, query_cols = weights[0].shape
    width = depth * CHUNKS
    out_weight = weights[CHUNKS + 2]
    loads_out = out_weight.ndim == 3
    out_cols = out_weight.shape[-1] // (CHUNKS if loads_out else 1)
    out_half = out_cols * CHUNKS // HALVES
    extra = [(query_cols, out_cols)] * CHUNKS if loads_out else []
    listed = lists.shape[1]
    rows = pieces[0].shape[0]
    tokens = rows * len(pieces) // HALVES
    vmem = pl.BlockSpec(memory_space=pltpu.VMEM)
    hbm = pl.BlockSpec(memory_space=pltpu.HBM)
    weights = [
        pltpu.with_memory_space_constraint(w, pltpu.HBM) if w.ndim == 3 else w for w in weights
    ]
    size = 2 * (width * (query_cols + 2 * HD) + query_cols * out_half * HALVES)
    return pl.pallas_call(
        functools.partial(
            layer_kernel, len(pieces), cache[0].shape[1] // BLOCK, device_rows, targets
        ),
        out_shape=[
            pltpu.VMEM(shape, jnp.bfloat16) for shape in [(r, out_half) for r in out_rows] + extra
        ],
        in_specs=[pl.BlockSpec(memory_space=pltpu.SMEM)] * 2
        + [vmem] * len(pieces)
        + [hbm if w.ndim == 3 else vmem for w in weights]
        + [hbm] * 2
        + [vmem] * 3,
        out_specs=[vmem] * (len(out_rows) + len(extra)),
        scratch_shapes=[
            pltpu.VMEM((listed * BLOCK, HD), jnp.bfloat16),
            pltpu.VMEM((listed * BLOCK, HD), jnp.bfloat16),
            pltpu.VMEM((tokens, query_cols), jnp.bfloat16),
            pltpu.SemaphoreType.DMA((2, listed - 1)),
            pltpu.SemaphoreType.DMA((CHUNKS,)),
        ],
        compiler_params=pltpu.CompilerParams(vmem_limit_bytes=10 << 20),
        cost_estimate=pl.CostEstimate(
            flops=tokens * size, bytes_accessed=size, transcendentals=tokens * listed * BLOCK * 8
        ),
        name="attention_sublayer",
    )(
        lists,
        place,
        *pieces,
        *weights,
        *[pltpu.with_memory_space_constraint(c, pltpu.HBM) for c in cache],
        *tables,
    )


def named(body, *args):
    bound = functools.partial(body, *args)
    bound.__name__ = body.__name__
    return bound


def chip_bits():
    return [1 << b for b in range(1, (lax.axis_size("head") - 1).bit_length())]


def small_call(body, shapes, *args):
    vmem = pl.BlockSpec(memory_space=pltpu.VMEM)
    size = sum(a.size * a.dtype.itemsize for a in args)
    return pl.pallas_call(
        body,
        out_shape=[pltpu.VMEM(shape, dtype) for shape, dtype in shapes],
        in_specs=[vmem if a.ndim > 1 else pl.BlockSpec(memory_space=pltpu.SMEM) for a in args],
        out_specs=[vmem] * len(shapes),
        compiler_params=pltpu.CompilerParams(vmem_limit_bytes=1 << 20),
        cost_estimate=pl.CostEstimate(flops=size, bytes_accessed=2 * size, transcendentals=0),
        name=body.__name__,
    )(*args)


def first_sum(own_ref, other_ref, kept_ref, *sent_refs):
    start = kept_ref.shape[0]
    kept_ref[...] = own_ref[:start].astype(jnp.float32) + other_ref[:start].astype(jnp.float32)
    for ref in sent_refs:
        part = slice(start, start + ref.shape[0])
        ref[...] = (
            own_ref[part].astype(jnp.float32) + other_ref[part].astype(jnp.float32)
        ).astype(ref.dtype)
        start = part.stop


def sum_on(kept_ref, other_ref, *sent_refs):
    start = 0
    skipped = kept_ref.shape[0] - other_ref.shape[0]
    for ref in sent_refs:
        size = ref.shape[0]
        kept = kept_ref[skipped + start : skipped + start + size]
        ref[...] = (kept + other_ref[start : start + size].astype(jnp.float32)).astype(ref.dtype)
        start += size


def sum_kept(kept_ref, other_ref, new_ref):
    new_ref[...] = kept_ref[: new_ref.shape[0]] + other_ref[...].astype(jnp.float32)


def last_sum(count, step, place_ref, *refs):
    states, kept, others = refs[:count], refs[count : 2 * count], refs[2 * count : 3 * count]
    rest = refs[3 * count :]
    output, outs = rest[-1], rest[-1 - count : -1] if len(rest) > count else ()
    earlier = rest[0] if step else None
    half = states[0].shape[1]
    for i in range(count):
        new = states[i][...].astype(jnp.float32) + kept[i][...] + others[i][...].astype(jnp.float32)
        new = new.astype(jnp.bfloat16)
        if outs:
            outs[i][...] = new
        part = slice(i * half, (i + 1) * half)
        if step:
            new = jnp.where(place_ref[0] == step, new, earlier[:, part])
        output[:, part] = new


def gather(states, orders, loads=()):
    halves = [{0: s} for s in states]
    loaded = []
    for phase in range(len(orders[0])):
        received = [
            {j ^ order[phase]: exchange(v, order[phase]) for j, v in blocks.items()}
            for blocks, order in zip(halves, orders)
        ]
        if phase < len(loads):
            received, weights = lax.optimization_barrier((received, loads[phase]))
            loaded += weights
        halves = [blocks | more for blocks, more in zip(halves, received)]
    for weights in loads[len(orders[0]) :]:
        loaded += weights
    halves = [blocks | {j ^ 1: exchange(v, 1) for j, v in blocks.items()} for blocks in halves]
    return [[blocks[j] for j in sorted(blocks)] for blocks in halves], loaded


def scatter_order(order, count):
    return sorted(range(0, count, 2), key=lambda j: [j & d for d in order])


def sent_shapes(blocks, rows, columns):
    cuts = [blocks // 2] * 2 if blocks > 1 else [1]
    return [((cut * rows, columns), jnp.bfloat16) for cut in cuts]


def scatter_half(even, odd, order, rows):
    columns = even.shape[1]
    blocks = even.shape[0] // rows // 2
    kept, *sent = small_call(
        first_sum,
        [((blocks * rows, columns), jnp.float32)] + sent_shapes(blocks, rows, columns),
        even,
        exchange(odd, 1),
    )
    for distance in order[:-1]:
        onward = exchange(sent[1], distance)
        staying = exchange(sent[0], distance)
        blocks //= 2
        sent = small_call(sum_on, sent_shapes(blocks, rows, columns), kept, onward)
        [kept] = small_call(sum_kept, [((blocks * rows, columns), jnp.float32)], kept, staying)
    return kept, exchange(sent[0], order[-1])


def on_device(
    prompt_states,
    norm_gain,
    query_weight,
    key_weight,
    value_weight,
    out_weight,
    cache_keys,
    cache_values,
    block_lists,
):
    sections = lax.axis_size("section")
    heads = lax.axis_size("head")
    section_index = lax.axis_index("section")
    head_index = lax.axis_index("head")
    rows, width = prompt_states.shape[1:]
    half = width // HALVES
    tokens = rows * heads
    prefix = cache_keys.shape[1]
    group_bits = (HD // key_weight.shape[2]).bit_length() - 1
    key_weight = join_columns(key_weight, group_bits, head_index)
    value_weight = join_columns(value_weight, group_bits, head_index)
    cache = (
        join_columns(cache_keys, group_bits, head_index),
        join_columns(cache_values, group_bits, head_index),
    )

    whole_tiles = rows % 16 == 0
    block_of = jnp.arange(heads, dtype=jnp.int32) ^ head_index
    positions = (
        prefix + block_of[:, None] * rows + jnp.arange(rows, dtype=jnp.int32)[None, :]
    ).reshape(tokens)
    inverse_freq = jnp.exp(-math.log(THETA) * jnp.arange(HD // 2, dtype=jnp.float32) * 2.0 / HD)
    angles = positions.astype(jnp.float32)[:, None] * inverse_freq[None, :]
    cosine, sine = jnp.cos(angles), jnp.sin(angles)
    tables = (
        norm_gain,
        jnp.concatenate([cosine, cosine], 1),
        jnp.concatenate([-sine, sine], 1),
    )
    place = jnp.stack([section_index, head_index]).astype(jnp.int32)
    projections = (query_weight, key_weight, value_weight)
    place, tables, projections, out_weight = lax.optimization_barrier(
        (place, tables, projections, out_weight)
    )

    orders = (chip_bits(), chip_bits()[::-1])
    if whole_tiles:
        targets = []
        for i, order in enumerate(orders):
            spots = {}
            for row, j in enumerate(scatter_order(order, heads)):
                spots |= {j: (2 * i, row * rows), j + 1: (2 * i + 1, row * rows)}
            targets.append(tuple(spots[j] for j in range(heads)))
        out_rows = [tokens // 2] * 2 * HALVES
    else:
        targets = [((i, 0),) for i in range(HALVES)]
        out_rows = [tokens] * HALVES

    loads = [
        load(projections[:1], ((1, CHUNKS, 0, CHUNKS // 2),)),
        load(projections, ((1, CHUNKS, CHUNKS // 2, CHUNKS), (1, 1, 0, 1), (1, 1, 0, 1))),
    ]
    states = [prompt_states[0, :, i * half : (i + 1) * half] for i in range(HALVES)]
    output = weights = None
    for step in range(sections):
        if step:
            states = [forward(s, step) for s in states]
        pieces, loaded = gather(states, orders, () if step else loads)
        weights = [*loaded, out_weight] if loaded else weights
        if not whole_tiles:
            pieces = [[jnp.concatenate(p, 0)] for p in pieces]
        partials = layer(
            sum(pieces, []), targets, out_rows, rows, weights, cache, block_lists, place, tables
        )
        made = len(out_rows)
        if not step:
            weights = [*weights[:-1], *partials[made:]]
        partials = partials[:made]
        if not whole_tiles:
            blocks = [jnp.split(p, heads, 0) for p in partials]
            partials = [
                jnp.concatenate([b[j + odd] for j in scatter_order(order, heads)], 0)
                for b, order in zip(blocks, orders)
                for odd in range(2)
            ]
        sums = [
            scatter_half(partials[2 * i], partials[2 * i + 1], order, rows)
            for i, order in enumerate(orders)
        ]
        kept, others = zip(*sums)
        goes_on = HALVES if step < sections - 1 else 0
        *states, output = small_call(
            named(last_sum, HALVES, step),
            [((rows, half), jnp.bfloat16)] * goes_on + [((rows, width), jnp.bfloat16)],
            place,
            *states,
            *kept,
            *others,
            *([output] if step else []),
        )
    return output[None, None]


def solution(mesh):
    return jax.shard_map(
        on_device,
        mesh=mesh,
        in_specs=(
            P(None, "head", None),
            P("section", None),
            P("section", None, "head"),
            P("section", None, "head"),
            P("section", None, "head"),
            P("section", "head", None),
            P("section", None, "head"),
            P("section", None, "head"),
            P(),
        ),
        out_specs=P("section", None, "head", None),
        check_vma=False,
    )
```

```python
import functools
import math

import jax
import jax.numpy as jnp
from jax import lax
from jax.experimental import pallas as pl
from jax.experimental.pallas import tpu as pltpu
from jax.sharding import PartitionSpec as P

HD = 128
BLOCK = 128
EPS = 1e-05
THETA = 500000.0
CHUNKS = 8
HALVES = 2
MASKED = -1e30


def exchange(value, distance):
    count = lax.axis_size("head")
    return lax.ppermute(value, "head", [(i, i ^ distance) for i in range(count)])


def forward(value, section):
    return lax.ppermute(value, "section", [(section - 1, section)])


def join_columns(part, group_bits, head_index):
    for bit in range(group_bits):
        other = exchange(part, 1 << bit)
        is_lower = head_index >> bit & 1 == 0
        part = jnp.where(
            is_lower, jnp.concatenate([part, other], -1), jnp.concatenate([other, part], -1)
        )
    return part


def loader_kernel(cuts, *refs):
    targets, sems = refs[len(cuts) : -1], refs[-1]
    sources = []
    for ref, (axis, count, first, last) in zip(refs, cuts):
        size = ref.shape[axis] // count
        for k in range(first, last):
            part = pl.ds(k * size, size)
            sources.append(ref.at[0, part, :] if axis == 1 else ref.at[0, :, part])
    copies = [
        pltpu.make_async_copy(source, target, sems.at[i])
        for i, (source, target) in enumerate(zip(sources, targets))
    ]
    for copy in copies:
        copy.start()
    for copy in copies:
        copy.wait()


def load(weights, cuts):
    shapes = []
    for weight, (axis, count, first, last) in zip(weights, cuts):
        shape = list(weight.shape)
        shape[axis] //= count
        shapes += [tuple(shape[1:])] * (last - first)
    size = sum(2 * math.prod(shape) for shape in shapes)
    return pl.pallas_call(
        functools.partial(loader_kernel, cuts),
        out_shape=[pltpu.VMEM(shape, jnp.bfloat16) for shape in shapes],
        in_specs=[pl.BlockSpec(memory_space=pltpu.HBM)] * len(weights),
        out_specs=[pl.BlockSpec(memory_space=pltpu.VMEM)] * len(shapes),
        scratch_shapes=[pltpu.SemaphoreType.DMA((len(shapes),))],
        compiler_params=pltpu.CompilerParams(vmem_limit_bytes=1 << 20),
        cost_estimate=pl.CostEstimate(flops=0, bytes_accessed=2 * size, transcendentals=0),
        name="load_weights",
    )(*[pltpu.with_memory_space_constraint(w, pltpu.HBM) for w in weights])


def layer_kernel(piece_count, cached_blocks, device_rows, targets, step, lists_ref, place_ref, *refs):
    pieces = refs[:piece_count]
    refs = refs[piece_count:]
    wq_refs, wk_ref, wv_ref = refs[:CHUNKS], refs[CHUNKS], refs[CHUNKS + 1]
    loads_out = len(refs[CHUNKS + 2].shape) == 3
    out_count = 1 if loads_out else CHUNKS
    wo_refs = refs[CHUNKS + 2 : CHUNKS + 2 + out_count]
    refs = refs[CHUNKS + 2 + out_count :]
    keys_hbm, values_hbm, gain_ref, cos_ref, sin_ref = refs[:5]
    outs = refs[5:-5]
    k_s, v_s, att_s, sem_c, sem_o = refs[-5:]
    out_copies = []
    if loads_out:
        source, outs, wo_refs = wo_refs[0], outs[:-CHUNKS], outs[-CHUNKS:]
        size = wo_refs[0].shape[1]
        for n, target in enumerate(wo_refs):
            part = source.at[0, :, pl.ds(n * size, size)]
            out_copies.append(pltpu.make_async_copy(part, target, sem_o.at[n]))
    rows, half = pieces[0].shape
    depth, query_cols = wq_refs[0].shape
    width = depth * CHUNKS
    row_blocks = piece_count * half // width
    out_cols = wo_refs[0].shape[1]
    out_half = out_cols * CHUNKS // HALVES
    query_heads = query_cols // HD
    listed = k_s.shape[0] // BLOCK

    cache_copies = []
    passed = lists_ref[0, 0] == cached_blocks
    for j in range(listed - 1):
        if j:
            passed = passed | (lists_ref[0, j] == cached_blocks)
        block = jnp.where(passed, lists_ref[0, j + 1], lists_ref[0, j])
        block = jnp.clip(block, 0, cached_blocks - 1)
        start = pl.multiple_of(block * BLOCK, BLOCK)
        for which, (source, target) in enumerate(((keys_hbm, k_s), (values_hbm, v_s))):
            cache_copies.append(
                pltpu.make_async_copy(
                    source.at[0, pl.ds(start, BLOCK), :],
                    target.at[pl.ds(j * BLOCK, BLOCK), :],
                    sem_c.at[which, j],
                )
            )
    for copy in out_copies:
        copy.start()
    active = place_ref[0] == step

    @pl.when(active)
    def _():
        for copy in cache_copies:
            copy.start()

        queries = new_keys = new_values = squares = 0.0
        for k in range(CHUNKS):
            part = slice(k * depth, (k + 1) * depth)
            which, inner = k * depth // half, k * depth % half
            x = jnp.concatenate(
                [
                    pieces[which * row_blocks + p][:, inner : inner + depth]
                    for p in range(row_blocks)
                ],
                0,
            ).astype(jnp.float32)
            squares += jnp.sum(x * x, -1, keepdims=True)
            x = (x * gain_ref[:, part]).astype(jnp.bfloat16)
            queries += jnp.dot(x, wq_refs[k][...], preferred_element_type=jnp.float32)
            new_keys += jnp.dot(x, wk_ref[part, :], preferred_element_type=jnp.float32)
            new_values += jnp.dot(x, wv_ref[part, :], preferred_element_type=jnp.float32)

        norm = lax.rsqrt(squares / width + EPS)
        cosine, sine = cos_ref[...], sin_ref[...]

        def rotated(value):
            return (value * cosine + pltpu.roll(value, HD // 2, 1) * sine).astype(jnp.bfloat16)

        new_keys = (new_keys * norm).astype(jnp.bfloat16).astype(jnp.float32)
        k_s[(listed - 1) * BLOCK :, :] = rotated(new_keys)
        v_s[(listed - 1) * BLOCK :, :] = (new_values * norm).astype(jnp.bfloat16)
        for copy in cache_copies:
            copy.wait()
        keys, values = k_s[...], v_s[...]

        def token(axis):
            index = lax.broadcasted_iota(jnp.int32, (BLOCK, BLOCK), axis)
            return (index // device_rows ^ place_ref[1]) * device_rows + index % device_rows

        allowed = token(1) <= token(0)
        factor = math.log2(math.e) / math.sqrt(HD)
        together = 2 if query_heads % 2 == 0 else 1
        allowed = jnp.concatenate([allowed] * together, 0)
        norms = jnp.concatenate([norm] * together, 0)
        cosine, sine = (jnp.concatenate([t] * together, 0) for t in (cosine, sine))
        for first in range(0, query_heads, together):
            heads = range(first, first + together)
            query = jnp.concatenate([queries[:, h * HD : (h + 1) * HD] for h in heads], 0)
            scores = lax.dot_general(
                rotated(query * norms),
                keys,
                (((1,), (1,)), ((), ())),
                preferred_element_type=jnp.float32,
            )
            scores = jnp.concatenate(
                [
                    scores[:, : (listed - 1) * BLOCK],
                    jnp.where(allowed, scores[:, (listed - 1) * BLOCK :], MASKED),
                ],
                1,
            )
            peak = jnp.max(scores, -1, keepdims=True)
            probabilities = jnp.exp2((scores - peak) * factor)
            totals = jnp.sum(probabilities, -1, keepdims=True)
            mixed = jnp.dot(
                probabilities.astype(jnp.bfloat16), values, preferred_element_type=jnp.float32
            )
            mixed = (mixed / totals).astype(jnp.bfloat16)
            for i, h in enumerate(heads):
                att_s[:, h * HD : (h + 1) * HD] = mixed[i * BLOCK : (i + 1) * BLOCK]

        attended = att_s[...]
        for n in range(CHUNKS):
            which, inner = n * out_cols // out_half, n * out_cols % out_half
            if loads_out:
                out_copies[n].wait()
            result = jnp.dot(attended, wo_refs[n][...], preferred_element_type=jnp.float32)
            result = result.astype(jnp.bfloat16)
            for p, (out, row) in enumerate(targets[which]):
                outs[out][row : row + rows, inner : inner + out_cols] = result[
                    p * rows : (p + 1) * rows
                ]

    @pl.when(jnp.logical_not(active))
    def _():
        for copy in out_copies:
            copy.wait()


def layer(step, pieces, targets, out_rows, device_rows, weights, cache, lists, place, tables):
    depth, query_cols = weights[0].shape
    width = depth * CHUNKS
    out_weight = weights[CHUNKS + 2]
    loads_out = out_weight.ndim == 3
    out_cols = out_weight.shape[-1] // (CHUNKS if loads_out else 1)
    out_half = out_cols * CHUNKS // HALVES
    extra = [(query_cols, out_cols)] * CHUNKS if loads_out else []
    listed = lists.shape[1]
    rows = pieces[0].shape[0]
    tokens = rows * len(pieces) * pieces[0].shape[1] // width
    vmem = pl.BlockSpec(memory_space=pltpu.VMEM)
    hbm = pl.BlockSpec(memory_space=pltpu.HBM)
    weights = [
        pltpu.with_memory_space_constraint(w, pltpu.HBM) if w.ndim == 3 else w for w in weights
    ]
    size = 2 * (width * (query_cols + 2 * HD) + query_cols * out_half * HALVES)
    return pl.pallas_call(
        functools.partial(
            layer_kernel, len(pieces), cache[0].shape[1] // BLOCK, device_rows, targets, step
        ),
        out_shape=[
            pltpu.VMEM(shape, jnp.bfloat16) for shape in [(r, out_half) for r in out_rows] + extra
        ],
        in_specs=[pl.BlockSpec(memory_space=pltpu.SMEM)] * 2
        + [vmem] * len(pieces)
        + [hbm if w.ndim == 3 else vmem for w in weights]
        + [hbm] * 2
        + [vmem] * 3,
        out_specs=[vmem] * (len(out_rows) + len(extra)),
        scratch_shapes=[
            pltpu.VMEM((listed * BLOCK, HD), jnp.bfloat16),
            pltpu.VMEM((listed * BLOCK, HD), jnp.bfloat16),
            pltpu.VMEM((tokens, query_cols), jnp.bfloat16),
            pltpu.SemaphoreType.DMA((2, listed - 1)),
            pltpu.SemaphoreType.DMA((CHUNKS,)),
        ],
        compiler_params=pltpu.CompilerParams(vmem_limit_bytes=10 << 20),
        cost_estimate=pl.CostEstimate(
            flops=tokens * size, bytes_accessed=size, transcendentals=tokens * listed * BLOCK * 8
        ),
        name="attention_sublayer",
    )(
        lists,
        place,
        *pieces,
        *weights,
        *[pltpu.with_memory_space_constraint(c, pltpu.HBM) for c in cache],
        *tables,
    )


def named(body, *args):
    bound = functools.partial(body, *args)
    bound.__name__ = body.__name__
    return bound


def chip_bits():
    return [1 << b for b in range(1, (lax.axis_size("head") - 1).bit_length())]


def small_call(body, shapes, *args):
    vmem = pl.BlockSpec(memory_space=pltpu.VMEM)
    size = sum(a.size * a.dtype.itemsize for a in args)
    return pl.pallas_call(
        body,
        out_shape=[pltpu.VMEM(shape, dtype) for shape, dtype in shapes],
        in_specs=[vmem if a.ndim > 1 else pl.BlockSpec(memory_space=pltpu.SMEM) for a in args],
        out_specs=[vmem] * len(shapes),
        compiler_params=pltpu.CompilerParams(vmem_limit_bytes=1 << 20),
        cost_estimate=pl.CostEstimate(flops=size, bytes_accessed=2 * size, transcendentals=0),
        name=body.__name__,
    )(*args)


def first_sum(own_ref, other_ref, kept_ref, *sent_refs):
    start = kept_ref.shape[0]
    kept_ref[...] = own_ref[:start].astype(jnp.float32) + other_ref[:start].astype(jnp.float32)
    for ref in sent_refs:
        part = slice(start, start + ref.shape[0])
        ref[...] = (
            own_ref[part].astype(jnp.float32) + other_ref[part].astype(jnp.float32)
        ).astype(ref.dtype)
        start = part.stop


def sum_on(kept_ref, other_ref, *sent_refs):
    start = 0
    skipped = kept_ref.shape[0] - other_ref.shape[0]
    for ref in sent_refs:
        size = ref.shape[0]
        kept = kept_ref[skipped + start : skipped + start + size]
        ref[...] = (kept + other_ref[start : start + size].astype(jnp.float32)).astype(ref.dtype)
        start += size


def sum_kept(kept_ref, other_ref, new_ref):
    new_ref[...] = kept_ref[: new_ref.shape[0]] + other_ref[...].astype(jnp.float32)


def last_sum(count, step, place_ref, *refs):
    states, kept, others = refs[:count], refs[count : 2 * count], refs[2 * count : 3 * count]
    rest = refs[3 * count :]
    output, outs = rest[-1], rest[-1 - count : -1] if len(rest) > count else ()
    earlier = rest[0] if step else None
    half = states[0].shape[1]
    for i in range(count):
        new = states[i][...].astype(jnp.float32) + kept[i][...] + others[i][...].astype(jnp.float32)
        new = new.astype(jnp.bfloat16)
        if outs:
            outs[i][...] = new
        part = slice(i * half, (i + 1) * half)
        if step:
            new = jnp.where(place_ref[0] == step, new, earlier[:, part])
        output[:, part] = new


def first_gather(own, loads):
    received = {j: exchange(own, j) for j in range(2, lax.axis_size("head"), 2)}
    received, weights = lax.optimization_barrier((received, loads))
    blocks = {0: own} | received
    blocks |= {j ^ 1: exchange(v, 1) for j, v in blocks.items()}
    return [[blocks[j] for j in sorted(blocks)]], sum(map(list, weights), [])


def gather(states, orders):
    halves = [{0: s} for s in states]
    for distances in zip(*orders):
        halves = [
            blocks | {j ^ distance: exchange(v, distance) for j, v in blocks.items()}
            for blocks, distance in zip(halves, distances)
        ]
    halves = [blocks | {j ^ 1: exchange(v, 1) for j, v in blocks.items()} for blocks in halves]
    return [[blocks[j] for j in sorted(blocks)] for blocks in halves]


def scatter_order(order, count):
    return sorted(range(0, count, 2), key=lambda j: [j & d for d in order])


def sent_shapes(blocks, rows, columns):
    cuts = [blocks // 2] * 2 if blocks > 1 else [1]
    return [((cut * rows, columns), jnp.bfloat16) for cut in cuts]


def scatter_half(even, odd, order, rows):
    columns = even.shape[1]
    blocks = even.shape[0] // rows // 2
    kept, *sent = small_call(
        first_sum,
        [((blocks * rows, columns), jnp.float32)] + sent_shapes(blocks, rows, columns),
        even,
        exchange(odd, 1),
    )
    for distance in order[:-1]:
        onward = exchange(sent[1], distance)
        staying = exchange(sent[0], distance)
        blocks //= 2
        sent = small_call(sum_on, sent_shapes(blocks, rows, columns), kept, onward)
        [kept] = small_call(sum_kept, [((blocks * rows, columns), jnp.float32)], kept, staying)
    return kept, exchange(sent[0], order[-1])


def on_device(
    prompt_states,
    norm_gain,
    query_weight,
    key_weight,
    value_weight,
    out_weight,
    cache_keys,
    cache_values,
    block_lists,
):
    sections = lax.axis_size("section")
    heads = lax.axis_size("head")
    section_index = lax.axis_index("section")
    head_index = lax.axis_index("head")
    rows, width = prompt_states.shape[1:]
    half = width // HALVES
    tokens = rows * heads
    prefix = cache_keys.shape[1]
    group_bits = (HD // key_weight.shape[2]).bit_length() - 1
    key_weight = join_columns(key_weight, group_bits, head_index)
    value_weight = join_columns(value_weight, group_bits, head_index)
    cache = (
        join_columns(cache_keys, group_bits, head_index),
        join_columns(cache_values, group_bits, head_index),
    )

    whole_tiles = rows % 16 == 0
    block_of = jnp.arange(heads, dtype=jnp.int32) ^ head_index
    positions = (
        prefix + block_of[:, None] * rows + jnp.arange(rows, dtype=jnp.int32)[None, :]
    ).reshape(tokens)
    inverse_freq = jnp.exp(-math.log(THETA) * jnp.arange(HD // 2, dtype=jnp.float32) * 2.0 / HD)
    angles = positions.astype(jnp.float32)[:, None] * inverse_freq[None, :]
    cosine, sine = jnp.cos(angles), jnp.sin(angles)
    tables = (
        norm_gain,
        jnp.concatenate([cosine, cosine], 1),
        jnp.concatenate([-sine, sine], 1),
    )
    place = jnp.stack([section_index, head_index]).astype(jnp.int32)
    projections = (query_weight, key_weight, value_weight)
    states = [prompt_states[0, :, i * half : (i + 1) * half] for i in range(HALVES)]
    states, place, tables, projections, out_weight = lax.optimization_barrier(
        (states, place, tables, projections, out_weight)
    )

    orders = (chip_bits(), chip_bits()[::-1])
    if whole_tiles:
        targets = []
        for i, order in enumerate(orders):
            spots = {}
            for row, j in enumerate(scatter_order(order, heads)):
                spots |= {j: (2 * i, row * rows), j + 1: (2 * i + 1, row * rows)}
            targets.append(tuple(spots[j] for j in range(heads)))
        out_rows = [tokens // 2] * 2 * HALVES
    else:
        targets = [((i, 0),) for i in range(HALVES)]
        out_rows = [tokens] * HALVES

    loads = [
        load(projections[:1], ((1, CHUNKS, 0, CHUNKS // 2),)),
        load(projections, ((1, CHUNKS, CHUNKS // 2, CHUNKS), (1, 1, 0, 1), (1, 1, 0, 1))),
    ]
    output = weights = None
    for step in range(sections):
        if step:
            states = [forward(s, step) for s in states]
        if step:
            pieces = gather(states, orders)
        else:
            pieces, loaded = first_gather(prompt_states[0], loads)
            weights = [*loaded, out_weight]
        if not whole_tiles:
            pieces = [[jnp.concatenate(p, 0)] for p in pieces]
        partials = layer(
            step, sum(pieces, []), targets, out_rows, rows, weights, cache, block_lists, place, tables
        )
        made = len(out_rows)
        if not step:
            weights = [*weights[:-1], *partials[made:]]
        partials = partials[:made]
        if not whole_tiles:
            blocks = [jnp.split(p, heads, 0) for p in partials]
            partials = [
                jnp.concatenate([b[j + odd] for j in scatter_order(order, heads)], 0)
                for b, order in zip(blocks, orders)
                for odd in range(2)
            ]
        sums = [
            scatter_half(partials[2 * i], partials[2 * i + 1], order, rows)
            for i, order in enumerate(orders)
        ]
        kept, others = zip(*sums)
        goes_on = HALVES if step < sections - 1 else 0
        *states, output = small_call(
            named(last_sum, HALVES, step),
            [((rows, half), jnp.bfloat16)] * goes_on + [((rows, width), jnp.bfloat16)],
            place,
            *states,
            *kept,
            *others,
            *([output] if step else []),
        )
    return output[None, None]


def solution(mesh):
    return jax.shard_map(
        on_device,
        mesh=mesh,
        in_specs=(
            P(None, "head", None),
            P("section", None),
            P("section", None, "head"),
            P("section", None, "head"),
            P("section", None, "head"),
            P("section", "head", None),
            P("section", None, "head"),
            P("section", None, "head"),
            P(),
        ),
        out_specs=P("section", None, "head", None),
        check_vma=False,
    )
```

```python
import functools
import math

import jax
import jax.numpy as jnp
from jax import lax
from jax.experimental import pallas as pl
from jax.experimental.pallas import tpu as pltpu
from jax.sharding import PartitionSpec as P

HD = 128
BLOCK = 128
EPS = 1e-05
THETA = 500000.0
CHUNKS = 8
HALVES = 2
MASKED = -1e30


def exchange(value, distance):
    count = lax.axis_size("head")
    return lax.ppermute(value, "head", [(i, i ^ distance) for i in range(count)])


def forward(value, section):
    return lax.ppermute(value, "section", [(section - 1, section)])


def join_columns(part, group_bits, head_index):
    for bit in range(group_bits):
        other = exchange(part, 1 << bit)
        is_lower = head_index >> bit & 1 == 0
        part = jnp.where(
            is_lower, jnp.concatenate([part, other], -1), jnp.concatenate([other, part], -1)
        )
    return part


def loader_kernel(cuts, *refs):
    targets, sems = refs[len(cuts) : -1], refs[-1]
    sources = []
    for ref, (axis, count, first, last) in zip(refs, cuts):
        size = ref.shape[axis] // count
        for k in range(first, last):
            part = pl.ds(k * size, size)
            sources.append(ref.at[0, part, :] if axis == 1 else ref.at[0, :, part])
    copies = [
        pltpu.make_async_copy(source, target, sems.at[i])
        for i, (source, target) in enumerate(zip(sources, targets))
    ]
    for copy in copies:
        copy.start()
    for copy in copies:
        copy.wait()


def load(weights, cuts):
    shapes = []
    for weight, (axis, count, first, last) in zip(weights, cuts):
        shape = list(weight.shape)
        shape[axis] //= count
        shapes += [tuple(shape[1:])] * (last - first)
    size = sum(2 * math.prod(shape) for shape in shapes)
    return pl.pallas_call(
        functools.partial(loader_kernel, cuts),
        out_shape=[pltpu.VMEM(shape, jnp.bfloat16) for shape in shapes],
        in_specs=[pl.BlockSpec(memory_space=pltpu.HBM)] * len(weights),
        out_specs=[pl.BlockSpec(memory_space=pltpu.VMEM)] * len(shapes),
        scratch_shapes=[pltpu.SemaphoreType.DMA((len(shapes),))],
        compiler_params=pltpu.CompilerParams(vmem_limit_bytes=1 << 20),
        cost_estimate=pl.CostEstimate(flops=0, bytes_accessed=2 * size, transcendentals=0),
        name="load_weights",
    )(*[pltpu.with_memory_space_constraint(w, pltpu.HBM) for w in weights])


def layer_kernel(piece_count, cached_blocks, device_rows, targets, step, lists_ref, place_ref, *refs):
    pieces = refs[:piece_count]
    refs = refs[piece_count:]
    wq_refs, wk_ref, wv_ref = refs[:CHUNKS], refs[CHUNKS], refs[CHUNKS + 1]
    loads_out = len(refs[CHUNKS + 2].shape) == 3
    out_count = 1 if loads_out else CHUNKS
    wo_refs = refs[CHUNKS + 2 : CHUNKS + 2 + out_count]
    refs = refs[CHUNKS + 2 + out_count :]
    keys_hbm, values_hbm, gain_ref, cos_ref, sin_ref = refs[:5]
    outs = refs[5:-5]
    k_s, v_s, att_s, sem_c, sem_o = refs[-5:]
    out_copies = []
    if loads_out:
        source, outs, wo_refs = wo_refs[0], outs[:-CHUNKS], outs[-CHUNKS:]
        size = wo_refs[0].shape[1]
        for n, target in enumerate(wo_refs):
            part = source.at[0, :, pl.ds(n * size, size)]
            out_copies.append(pltpu.make_async_copy(part, target, sem_o.at[n]))
    rows, half = pieces[0].shape
    depth, query_cols = wq_refs[0].shape
    width = depth * CHUNKS
    row_blocks = piece_count * half // width
    out_cols = wo_refs[0].shape[1]
    out_half = out_cols * CHUNKS // HALVES
    query_heads = query_cols // HD
    listed = k_s.shape[0] // BLOCK

    cache_copies = []
    passed = lists_ref[0, 0] == cached_blocks
    for j in range(listed - 1):
        if j:
            passed = passed | (lists_ref[0, j] == cached_blocks)
        block = jnp.where(passed, lists_ref[0, j + 1], lists_ref[0, j])
        block = jnp.clip(block, 0, cached_blocks - 1)
        start = pl.multiple_of(block * BLOCK, BLOCK)
        for which, (source, target) in enumerate(((keys_hbm, k_s), (values_hbm, v_s))):
            cache_copies.append(
                pltpu.make_async_copy(
                    source.at[0, pl.ds(start, BLOCK), :],
                    target.at[pl.ds(j * BLOCK, BLOCK), :],
                    sem_c.at[which, j],
                )
            )
    for copy in out_copies:
        copy.start()
    active = place_ref[0] == step

    @pl.when(active)
    def _():
        for copy in cache_copies:
            copy.start()

        queries = new_keys = new_values = squares = 0.0
        for k in range(CHUNKS):
            part = slice(k * depth, (k + 1) * depth)
            which, inner = k * depth // half, k * depth % half
            x = jnp.concatenate(
                [
                    pieces[which * row_blocks + p][:, inner : inner + depth]
                    for p in range(row_blocks)
                ],
                0,
            ).astype(jnp.float32)
            squares += jnp.sum(x * x, -1, keepdims=True)
            x = (x * gain_ref[:, part]).astype(jnp.bfloat16)
            queries += jnp.dot(x, wq_refs[k][...], preferred_element_type=jnp.float32)
            new_keys += jnp.dot(x, wk_ref[part, :], preferred_element_type=jnp.float32)
            new_values += jnp.dot(x, wv_ref[part, :], preferred_element_type=jnp.float32)

        norm = lax.rsqrt(squares / width + EPS)
        cosine, sine = cos_ref[...], sin_ref[...]

        def rotated(value):
            return (value * cosine + pltpu.roll(value, HD // 2, 1) * sine).astype(jnp.bfloat16)

        new_keys = (new_keys * norm).astype(jnp.bfloat16).astype(jnp.float32)
        k_s[(listed - 1) * BLOCK :, :] = rotated(new_keys)
        v_s[(listed - 1) * BLOCK :, :] = (new_values * norm).astype(jnp.bfloat16)
        for copy in cache_copies:
            copy.wait()
        keys, values = k_s[...], v_s[...]

        def token(axis):
            index = lax.broadcasted_iota(jnp.int32, (BLOCK, BLOCK), axis)
            return (index // device_rows ^ place_ref[1]) * device_rows + index % device_rows

        allowed = token(1) <= token(0)
        factor = math.log2(math.e) / math.sqrt(HD)
        together = 2 if query_heads % 2 == 0 else 1
        allowed = jnp.concatenate([allowed] * together, 0)
        norms = jnp.concatenate([norm] * together, 0)
        cosine, sine = (jnp.concatenate([t] * together, 0) for t in (cosine, sine))
        for first in range(0, query_heads, together):
            heads = range(first, first + together)
            query = jnp.concatenate([queries[:, h * HD : (h + 1) * HD] for h in heads], 0)
            scores = lax.dot_general(
                rotated(query * norms),
                keys,
                (((1,), (1,)), ((), ())),
                preferred_element_type=jnp.float32,
            )
            scores = jnp.concatenate(
                [
                    scores[:, : (listed - 1) * BLOCK],
                    jnp.where(allowed, scores[:, (listed - 1) * BLOCK :], MASKED),
                ],
                1,
            )
            peak = jnp.max(scores, -1, keepdims=True)
            probabilities = jnp.exp2((scores - peak) * factor)
            totals = jnp.sum(probabilities, -1, keepdims=True)
            mixed = jnp.dot(
                probabilities.astype(jnp.bfloat16), values, preferred_element_type=jnp.float32
            )
            mixed = (mixed / totals).astype(jnp.bfloat16)
            for i, h in enumerate(heads):
                att_s[:, h * HD : (h + 1) * HD] = mixed[i * BLOCK : (i + 1) * BLOCK]

        attended = att_s[...]
        for n in range(CHUNKS):
            which, inner = n * out_cols // out_half, n * out_cols % out_half
            if loads_out:
                out_copies[n].wait()
            result = jnp.dot(attended, wo_refs[n][...], preferred_element_type=jnp.float32)
            result = result.astype(jnp.bfloat16)
            for p, (out, row) in enumerate(targets[which]):
                outs[out][row : row + rows, inner : inner + out_cols] = result[
                    p * rows : (p + 1) * rows
                ]

    @pl.when(jnp.logical_not(active))
    def _():
        for copy in out_copies:
            copy.wait()


def layer(step, pieces, targets, out_rows, device_rows, weights, cache, lists, place, tables):
    depth, query_cols = weights[0].shape
    width = depth * CHUNKS
    out_weight = weights[CHUNKS + 2]
    loads_out = out_weight.ndim == 3
    out_cols = out_weight.shape[-1] // (CHUNKS if loads_out else 1)
    out_half = out_cols * CHUNKS // HALVES
    extra = [(query_cols, out_cols)] * CHUNKS if loads_out else []
    listed = lists.shape[1]
    rows = pieces[0].shape[0]
    tokens = rows * len(pieces) * pieces[0].shape[1] // width
    vmem = pl.BlockSpec(memory_space=pltpu.VMEM)
    hbm = pl.BlockSpec(memory_space=pltpu.HBM)
    weights = [
        pltpu.with_memory_space_constraint(w, pltpu.HBM) if w.ndim == 3 else w for w in weights
    ]
    size = 2 * (width * (query_cols + 2 * HD) + query_cols * out_half * HALVES)
    return pl.pallas_call(
        functools.partial(
            layer_kernel, len(pieces), cache[0].shape[1] // BLOCK, device_rows, targets, step
        ),
        out_shape=[
            pltpu.VMEM(shape, jnp.bfloat16) for shape in [(r, out_half) for r in out_rows] + extra
        ],
        in_specs=[pl.BlockSpec(memory_space=pltpu.SMEM)] * 2
        + [vmem] * len(pieces)
        + [hbm if w.ndim == 3 else vmem for w in weights]
        + [hbm] * 2
        + [vmem] * 3,
        out_specs=[vmem] * (len(out_rows) + len(extra)),
        scratch_shapes=[
            pltpu.VMEM((listed * BLOCK, HD), jnp.bfloat16),
            pltpu.VMEM((listed * BLOCK, HD), jnp.bfloat16),
            pltpu.VMEM((tokens, query_cols), jnp.bfloat16),
            pltpu.SemaphoreType.DMA((2, listed - 1)),
            pltpu.SemaphoreType.DMA((CHUNKS,)),
        ],
        compiler_params=pltpu.CompilerParams(vmem_limit_bytes=10 << 20),
        cost_estimate=pl.CostEstimate(
            flops=tokens * size, bytes_accessed=size, transcendentals=tokens * listed * BLOCK * 8
        ),
        name="attention_sublayer",
    )(
        lists,
        place,
        *pieces,
        *weights,
        *[pltpu.with_memory_space_constraint(c, pltpu.HBM) for c in cache],
        *tables,
    )


def named(body, *args):
    bound = functools.partial(body, *args)
    bound.__name__ = body.__name__
    return bound


def chip_bits():
    return [1 << b for b in range(1, (lax.axis_size("head") - 1).bit_length())]


def small_call(body, shapes, *args):
    vmem = pl.BlockSpec(memory_space=pltpu.VMEM)
    size = sum(a.size * a.dtype.itemsize for a in args)
    return pl.pallas_call(
        body,
        out_shape=[pltpu.VMEM(shape, dtype) for shape, dtype in shapes],
        in_specs=[vmem if a.ndim > 1 else pl.BlockSpec(memory_space=pltpu.SMEM) for a in args],
        out_specs=[vmem] * len(shapes),
        compiler_params=pltpu.CompilerParams(vmem_limit_bytes=1 << 20),
        cost_estimate=pl.CostEstimate(flops=size, bytes_accessed=2 * size, transcendentals=0),
        name=body.__name__,
    )(*args)


def first_sum(own_ref, other_ref, kept_ref, *sent_refs):
    start = kept_ref.shape[0]
    kept_ref[...] = own_ref[:start].astype(jnp.float32) + other_ref[:start].astype(jnp.float32)
    for ref in sent_refs:
        part = slice(start, start + ref.shape[0])
        ref[...] = (
            own_ref[part].astype(jnp.float32) + other_ref[part].astype(jnp.float32)
        ).astype(ref.dtype)
        start = part.stop


def sum_on(kept_ref, other_ref, *sent_refs):
    start = 0
    skipped = kept_ref.shape[0] - other_ref.shape[0]
    for ref in sent_refs:
        size = ref.shape[0]
        kept = kept_ref[skipped + start : skipped + start + size]
        ref[...] = (kept + other_ref[start : start + size].astype(jnp.float32)).astype(ref.dtype)
        start += size


def sum_kept(kept_ref, other_ref, new_ref):
    new_ref[...] = kept_ref[: new_ref.shape[0]] + other_ref[...].astype(jnp.float32)


def last_sum(*refs):
    count = len(refs) // 4
    for states, kept, other, new in zip(*(refs[i * count : (i + 1) * count] for i in range(4))):
        total = states[...].astype(jnp.float32) + kept[...] + other[...].astype(jnp.float32)
        new[...] = total.astype(new.dtype)


def keep_output(count, step, place_ref, *refs):
    states, output = refs[:count], refs[-1]
    half = states[0].shape[1]
    for i in range(count):
        part = slice(i * half, (i + 1) * half)
        new = states[i][...]
        if step:
            new = jnp.where(place_ref[0] == step, new, refs[count][:, part])
        output[:, part] = new


def first_gather(own, loads):
    received = {j: exchange(own, j) for j in range(2, lax.axis_size("head"), 2)}
    received, weights = lax.optimization_barrier((received, loads))
    blocks = {0: own} | received
    blocks |= {j ^ 1: exchange(v, 1) for j, v in blocks.items()}
    return [[blocks[j] for j in sorted(blocks)]], sum(map(list, weights), [])


def gather(states, orders):
    halves = [{0: s} for s in states]
    for distances in zip(*orders):
        halves = [
            blocks | {j ^ distance: exchange(v, distance) for j, v in blocks.items()}
            for blocks, distance in zip(halves, distances)
        ]
    halves = [blocks | {j ^ 1: exchange(v, 1) for j, v in blocks.items()} for blocks in halves]
    return [[blocks[j] for j in sorted(blocks)] for blocks in halves]


def scatter_order(order, count):
    return sorted(range(0, count, 2), key=lambda j: [j & d for d in order])


def sent_shapes(blocks, rows, columns):
    cuts = [blocks // 2] * 2 if blocks > 1 else [1]
    return [((cut * rows, columns), jnp.bfloat16) for cut in cuts]


def scatter_half(even, odd, order, rows):
    columns = even.shape[1]
    blocks = even.shape[0] // rows // 2
    kept, *sent = small_call(
        first_sum,
        [((blocks * rows, columns), jnp.float32)] + sent_shapes(blocks, rows, columns),
        even,
        exchange(odd, 1),
    )
    for distance in order[:-1]:
        onward = exchange(sent[1], distance)
        staying = exchange(sent[0], distance)
        blocks //= 2
        sent = small_call(sum_on, sent_shapes(blocks, rows, columns), kept, onward)
        [kept] = small_call(sum_kept, [((blocks * rows, columns), jnp.float32)], kept, staying)
    return kept, exchange(sent[0], order[-1])


def on_device(
    prompt_states,
    norm_gain,
    query_weight,
    key_weight,
    value_weight,
    out_weight,
    cache_keys,
    cache_values,
    block_lists,
):
    sections = lax.axis_size("section")
    heads = lax.axis_size("head")
    section_index = lax.axis_index("section")
    head_index = lax.axis_index("head")
    rows, width = prompt_states.shape[1:]
    half = width // HALVES
    tokens = rows * heads
    prefix = cache_keys.shape[1]
    group_bits = (HD // key_weight.shape[2]).bit_length() - 1
    key_weight = join_columns(key_weight, group_bits, head_index)
    value_weight = join_columns(value_weight, group_bits, head_index)
    cache = (
        join_columns(cache_keys, group_bits, head_index),
        join_columns(cache_values, group_bits, head_index),
    )

    whole_tiles = rows % 16 == 0
    block_of = jnp.arange(heads, dtype=jnp.int32) ^ head_index
    positions = (
        prefix + block_of[:, None] * rows + jnp.arange(rows, dtype=jnp.int32)[None, :]
    ).reshape(tokens)
    inverse_freq = jnp.exp(-math.log(THETA) * jnp.arange(HD // 2, dtype=jnp.float32) * 2.0 / HD)
    angles = positions.astype(jnp.float32)[:, None] * inverse_freq[None, :]
    cosine, sine = jnp.cos(angles), jnp.sin(angles)
    tables = (
        norm_gain,
        jnp.concatenate([cosine, cosine], 1),
        jnp.concatenate([-sine, sine], 1),
    )
    place = jnp.stack([section_index, head_index]).astype(jnp.int32)
    projections = (query_weight, key_weight, value_weight)
    states = [prompt_states[0, :, i * half : (i + 1) * half] for i in range(HALVES)]
    states, place, tables, projections, out_weight = lax.optimization_barrier(
        (states, place, tables, projections, out_weight)
    )

    orders = (chip_bits(), chip_bits()[::-1])
    if whole_tiles:
        targets = []
        for i, order in enumerate(orders):
            spots = {}
            for row, j in enumerate(scatter_order(order, heads)):
                spots |= {j: (2 * i, row * rows), j + 1: (2 * i + 1, row * rows)}
            targets.append(tuple(spots[j] for j in range(heads)))
        out_rows = [tokens // 2] * 2 * HALVES
    else:
        targets = [((i, 0),) for i in range(HALVES)]
        out_rows = [tokens] * HALVES

    loads = [
        load(projections[:1], ((1, CHUNKS, 0, CHUNKS // 2),)),
        load(projections, ((1, CHUNKS, CHUNKS // 2, CHUNKS), (1, 1, 0, 1), (1, 1, 0, 1))),
    ]
    output = weights = None
    for step in range(sections):
        if step:
            states = [forward(s, step) for s in states]
        if step:
            pieces = gather(states, orders)
        else:
            pieces, loaded = first_gather(prompt_states[0], loads)
            weights = [*loaded, out_weight]
        if not whole_tiles:
            pieces = [[jnp.concatenate(p, 0)] for p in pieces]
        partials = layer(
            step, sum(pieces, []), targets, out_rows, rows, weights, cache, block_lists, place, tables
        )
        made = len(out_rows)
        if not step:
            weights = [*weights[:-1], *partials[made:]]
        partials = partials[:made]
        if not whole_tiles:
            blocks = [jnp.split(p, heads, 0) for p in partials]
            partials = [
                jnp.concatenate([b[j + odd] for j in scatter_order(order, heads)], 0)
                for b, order in zip(blocks, orders)
                for odd in range(2)
            ]
        sums = [
            scatter_half(partials[2 * i], partials[2 * i + 1], order, rows)
            for i, order in enumerate(orders)
        ]
        kept, others = zip(*sums)
        states = small_call(
            last_sum, [((rows, half), jnp.bfloat16)] * HALVES, *states, *kept, *others
        )
        [output] = small_call(
            named(keep_output, HALVES, step),
            [((rows, width), jnp.bfloat16)],
            place,
            *states,
            *([output] if step else []),
        )
    return output[None, None]


def solution(mesh):
    return jax.shard_map(
        on_device,
        mesh=mesh,
        in_specs=(
            P(None, "head", None),
            P("section", None),
            P("section", None, "head"),
            P("section", None, "head"),
            P("section", None, "head"),
            P("section", "head", None),
            P("section", None, "head"),
            P("section", None, "head"),
            P(),
        ),
        out_specs=P("section", None, "head", None),
        check_vma=False,
    )
```

```python
import functools
import math

import jax
import jax.numpy as jnp
from jax import lax
from jax.experimental import pallas as pl
from jax.experimental.pallas import tpu as pltpu
from jax.sharding import PartitionSpec as P

HD = 128
BLOCK = 128
EPS = 1e-05
THETA = 500000.0
CHUNKS = 8
HALVES = 2
MASKED = -1e30


def exchange(value, distance):
    count = lax.axis_size("head")
    return lax.ppermute(value, "head", [(i, i ^ distance) for i in range(count)])


def forward(value, section):
    return lax.ppermute(value, "section", [(section - 1, section)])


def join_columns(part, group_bits, head_index):
    for bit in range(group_bits):
        other = exchange(part, 1 << bit)
        is_lower = head_index >> bit & 1 == 0
        part = jnp.where(
            is_lower, jnp.concatenate([part, other], -1), jnp.concatenate([other, part], -1)
        )
    return part


def loader_kernel(cuts, *refs):
    targets, sems = refs[len(cuts) : -1], refs[-1]
    sources = []
    for ref, (axis, count, first, last) in zip(refs, cuts):
        size = ref.shape[axis] // count
        for k in range(first, last):
            part = pl.ds(k * size, size)
            sources.append(ref.at[0, part, :] if axis == 1 else ref.at[0, :, part])
    copies = [
        pltpu.make_async_copy(source, target, sems.at[i])
        for i, (source, target) in enumerate(zip(sources, targets))
    ]
    for copy in copies:
        copy.start()
    for copy in copies:
        copy.wait()


def load(weights, cuts):
    shapes = []
    for weight, (axis, count, first, last) in zip(weights, cuts):
        shape = list(weight.shape)
        shape[axis] //= count
        shapes += [tuple(shape[1:])] * (last - first)
    size = sum(2 * math.prod(shape) for shape in shapes)
    return pl.pallas_call(
        functools.partial(loader_kernel, cuts),
        out_shape=[pltpu.VMEM(shape, jnp.bfloat16) for shape in shapes],
        in_specs=[pl.BlockSpec(memory_space=pltpu.HBM)] * len(weights),
        out_specs=[pl.BlockSpec(memory_space=pltpu.VMEM)] * len(shapes),
        scratch_shapes=[pltpu.SemaphoreType.DMA((len(shapes),))],
        compiler_params=pltpu.CompilerParams(vmem_limit_bytes=1 << 20),
        cost_estimate=pl.CostEstimate(flops=0, bytes_accessed=2 * size, transcendentals=0),
        name="load_weights",
    )(*[pltpu.with_memory_space_constraint(w, pltpu.HBM) for w in weights])


def layer_kernel(piece_count, cached_blocks, device_rows, targets, step, lists_ref, place_ref, *refs):
    pieces = refs[:piece_count]
    refs = refs[piece_count:]
    wq_refs, wk_ref, wv_ref = refs[:CHUNKS], refs[CHUNKS], refs[CHUNKS + 1]
    loads_out = len(refs[CHUNKS + 2].shape) == 3
    out_count = 1 if loads_out else CHUNKS
    wo_refs = refs[CHUNKS + 2 : CHUNKS + 2 + out_count]
    refs = refs[CHUNKS + 2 + out_count :]
    keys_hbm, values_hbm, gain_ref, cos_ref, sin_ref = refs[:5]
    outs = refs[5:-5]
    k_s, v_s, att_s, sem_c, sem_o = refs[-5:]
    out_copies = []
    if loads_out:
        source, outs, wo_refs = wo_refs[0], outs[:-CHUNKS], outs[-CHUNKS:]
        size = wo_refs[0].shape[1]
        for n, target in enumerate(wo_refs):
            part = source.at[0, :, pl.ds(n * size, size)]
            out_copies.append(pltpu.make_async_copy(part, target, sem_o.at[n]))
    rows, half = pieces[0].shape
    depth, query_cols = wq_refs[0].shape
    width = depth * CHUNKS
    row_blocks = piece_count * half // width
    out_cols = wo_refs[0].shape[1]
    out_half = out_cols * CHUNKS // HALVES
    query_heads = query_cols // HD
    listed = k_s.shape[0] // BLOCK

    cache_copies = []
    passed = lists_ref[0, 0] == cached_blocks
    for j in range(listed - 1):
        if j:
            passed = passed | (lists_ref[0, j] == cached_blocks)
        block = jnp.where(passed, lists_ref[0, j + 1], lists_ref[0, j])
        block = jnp.clip(block, 0, cached_blocks - 1)
        start = pl.multiple_of(block * BLOCK, BLOCK)
        for which, (source, target) in enumerate(((keys_hbm, k_s), (values_hbm, v_s))):
            cache_copies.append(
                pltpu.make_async_copy(
                    source.at[0, pl.ds(start, BLOCK), :],
                    target.at[pl.ds(j * BLOCK, BLOCK), :],
                    sem_c.at[which, j],
                )
            )
    for copy in out_copies:
        copy.start()
    active = place_ref[0] == step

    @pl.when(active)
    def _():
        for copy in cache_copies:
            copy.start()

        queries = new_keys = new_values = squares = 0.0
        for k in range(CHUNKS):
            part = slice(k * depth, (k + 1) * depth)
            which, inner = k * depth // half, k * depth % half
            x = jnp.concatenate(
                [
                    pieces[which * row_blocks + p][:, inner : inner + depth]
                    for p in range(row_blocks)
                ],
                0,
            ).astype(jnp.float32)
            squares += jnp.sum(x * x, -1, keepdims=True)
            x = (x * gain_ref[:, part]).astype(jnp.bfloat16)
            queries += jnp.dot(x, wq_refs[k][...], preferred_element_type=jnp.float32)
            new_keys += jnp.dot(x, wk_ref[part, :], preferred_element_type=jnp.float32)
            new_values += jnp.dot(x, wv_ref[part, :], preferred_element_type=jnp.float32)

        norm = lax.rsqrt(squares / width + EPS)
        cosine, sine = cos_ref[...], sin_ref[...]

        def rotated(value):
            return (value * cosine + pltpu.roll(value, HD // 2, 1) * sine).astype(jnp.bfloat16)

        new_keys = (new_keys * norm).astype(jnp.bfloat16).astype(jnp.float32)
        k_s[(listed - 1) * BLOCK :, :] = rotated(new_keys)
        v_s[(listed - 1) * BLOCK :, :] = (new_values * norm).astype(jnp.bfloat16)
        for copy in cache_copies:
            copy.wait()
        keys, values = k_s[...], v_s[...]

        def token(axis):
            index = lax.broadcasted_iota(jnp.int32, (BLOCK, BLOCK), axis)
            return (index // device_rows ^ place_ref[1]) * device_rows + index % device_rows

        allowed = token(1) <= token(0)
        factor = math.log2(math.e) / math.sqrt(HD)
        together = 2 if query_heads % 2 == 0 else 1
        allowed = jnp.concatenate([allowed] * together, 0)
        norms = jnp.concatenate([norm] * together, 0)
        cosine, sine = (jnp.concatenate([t] * together, 0) for t in (cosine, sine))
        for first in range(0, query_heads, together):
            heads = range(first, first + together)
            query = jnp.concatenate([queries[:, h * HD : (h + 1) * HD] for h in heads], 0)
            scores = lax.dot_general(
                rotated(query * norms),
                keys,
                (((1,), (1,)), ((), ())),
                preferred_element_type=jnp.float32,
            )
            scores = jnp.concatenate(
                [
                    scores[:, : (listed - 1) * BLOCK],
                    jnp.where(allowed, scores[:, (listed - 1) * BLOCK :], MASKED),
                ],
                1,
            )
            peak = jnp.max(scores, -1, keepdims=True)
            probabilities = jnp.exp2((scores - peak) * factor)
            totals = jnp.sum(probabilities, -1, keepdims=True)
            mixed = jnp.dot(
                probabilities.astype(jnp.bfloat16), values, preferred_element_type=jnp.float32
            )
            mixed = (mixed / totals).astype(jnp.bfloat16)
            for i, h in enumerate(heads):
                att_s[:, h * HD : (h + 1) * HD] = mixed[i * BLOCK : (i + 1) * BLOCK]

        attended = att_s[...]
        for n in range(CHUNKS):
            which, inner = n * out_cols // out_half, n * out_cols % out_half
            if loads_out:
                out_copies[n].wait()
            result = jnp.dot(attended, wo_refs[n][...], preferred_element_type=jnp.float32)
            result = result.astype(jnp.bfloat16)
            for p, (out, row) in enumerate(targets[which]):
                outs[out][row : row + rows, inner : inner + out_cols] = result[
                    p * rows : (p + 1) * rows
                ]

    @pl.when(jnp.logical_not(active))
    def _():
        for copy in out_copies:
            copy.wait()


def layer(step, pieces, targets, out_rows, device_rows, weights, cache, lists, place, tables):
    depth, query_cols = weights[0].shape
    width = depth * CHUNKS
    out_weight = weights[CHUNKS + 2]
    loads_out = out_weight.ndim == 3
    out_cols = out_weight.shape[-1] // (CHUNKS if loads_out else 1)
    out_half = out_cols * CHUNKS // HALVES
    extra = [(query_cols, out_cols)] * CHUNKS if loads_out else []
    listed = lists.shape[1]
    rows = pieces[0].shape[0]
    tokens = rows * len(pieces) * pieces[0].shape[1] // width
    vmem = pl.BlockSpec(memory_space=pltpu.VMEM)
    hbm = pl.BlockSpec(memory_space=pltpu.HBM)
    weights = [
        pltpu.with_memory_space_constraint(w, pltpu.HBM) if w.ndim == 3 else w for w in weights
    ]
    size = 2 * (width * (query_cols + 2 * HD) + query_cols * out_half * HALVES)
    return pl.pallas_call(
        functools.partial(
            layer_kernel, len(pieces), cache[0].shape[1] // BLOCK, device_rows, targets, step
        ),
        out_shape=[
            pltpu.VMEM(shape, jnp.bfloat16) for shape in [(r, out_half) for r in out_rows] + extra
        ],
        in_specs=[pl.BlockSpec(memory_space=pltpu.SMEM)] * 2
        + [vmem] * len(pieces)
        + [hbm if w.ndim == 3 else vmem for w in weights]
        + [hbm] * 2
        + [vmem] * 3,
        out_specs=[vmem] * (len(out_rows) + len(extra)),
        scratch_shapes=[
            pltpu.VMEM((listed * BLOCK, HD), jnp.bfloat16),
            pltpu.VMEM((listed * BLOCK, HD), jnp.bfloat16),
            pltpu.VMEM((tokens, query_cols), jnp.bfloat16),
            pltpu.SemaphoreType.DMA((2, listed - 1)),
            pltpu.SemaphoreType.DMA((CHUNKS,)),
        ],
        compiler_params=pltpu.CompilerParams(vmem_limit_bytes=10 << 20),
        cost_estimate=pl.CostEstimate(
            flops=tokens * size, bytes_accessed=size, transcendentals=tokens * listed * BLOCK * 8
        ),
        name="attention_sublayer",
    )(
        lists,
        place,
        *pieces,
        *weights,
        *[pltpu.with_memory_space_constraint(c, pltpu.HBM) for c in cache],
        *tables,
    )


def named(body, *args):
    bound = functools.partial(body, *args)
    bound.__name__ = body.__name__
    return bound


def chip_bits():
    return [1 << b for b in range(1, (lax.axis_size("head") - 1).bit_length())]


def small_call(body, shapes, *args):
    vmem = pl.BlockSpec(memory_space=pltpu.VMEM)
    size = sum(a.size * a.dtype.itemsize for a in args)
    return pl.pallas_call(
        body,
        out_shape=[pltpu.VMEM(shape, dtype) for shape, dtype in shapes],
        in_specs=[vmem if a.ndim > 1 else pl.BlockSpec(memory_space=pltpu.SMEM) for a in args],
        out_specs=[vmem] * len(shapes),
        compiler_params=pltpu.CompilerParams(vmem_limit_bytes=1 << 20),
        cost_estimate=pl.CostEstimate(flops=size, bytes_accessed=2 * size, transcendentals=0),
        name=body.__name__,
    )(*args)


def first_sum(own_ref, other_ref, kept_ref, *sent_refs):
    start = kept_ref.shape[0]
    kept_ref[...] = own_ref[:start].astype(jnp.float32) + other_ref[:start].astype(jnp.float32)
    for ref in sent_refs:
        part = slice(start, start + ref.shape[0])
        ref[...] = (
            own_ref[part].astype(jnp.float32) + other_ref[part].astype(jnp.float32)
        ).astype(ref.dtype)
        start = part.stop


def sum_on(kept_ref, other_ref, *sent_refs):
    start = 0
    skipped = kept_ref.shape[0] - other_ref.shape[0]
    for ref in sent_refs:
        size = ref.shape[0]
        kept = kept_ref[skipped + start : skipped + start + size]
        ref[...] = (kept + other_ref[start : start + size].astype(jnp.float32)).astype(ref.dtype)
        start += size


def sum_kept(kept_ref, other_ref, new_ref):
    new_ref[...] = kept_ref[: new_ref.shape[0]] + other_ref[...].astype(jnp.float32)


def last_sum(*refs):
    count = len(refs) // 4
    for states, kept, other, new in zip(*(refs[i * count : (i + 1) * count] for i in range(4))):
        total = states[...].astype(jnp.float32) + kept[...] + other[...].astype(jnp.float32)
        new[...] = total.astype(new.dtype)


def keep_output(count, step, place_ref, *refs):
    states, output = refs[:count], refs[-1]
    half = states[0].shape[1]
    for i in range(count):
        part = slice(i * half, (i + 1) * half)
        new = states[i][...]
        if step:
            new = jnp.where(place_ref[0] == step, new, refs[count][:, part])
        output[:, part] = new


def first_gather(own, loads):
    received = {j: exchange(own, j) for j in range(2, lax.axis_size("head"), 2)}
    received, weights = lax.optimization_barrier((received, loads))
    blocks = {0: own} | received
    blocks |= {j ^ 1: exchange(v, 1) for j, v in blocks.items()}
    return [[blocks[j] for j in sorted(blocks)]], sum(map(list, weights), [])


def gather(states, orders):
    halves = [{0: s} for s in states]
    for distances in zip(*orders):
        halves = [
            blocks | {j ^ distance: exchange(v, distance) for j, v in blocks.items()}
            for blocks, distance in zip(halves, distances)
        ]
    halves = [blocks | {j ^ 1: exchange(v, 1) for j, v in blocks.items()} for blocks in halves]
    return [[blocks[j] for j in sorted(blocks)] for blocks in halves]


def scatter_order(order, count):
    return sorted(range(0, count, 2), key=lambda j: [j & d for d in order])


def sent_shapes(blocks, rows, columns):
    cuts = [blocks // 2] * 2 if blocks > 1 else [1]
    return [((cut * rows, columns), jnp.bfloat16) for cut in cuts]


def scatter_half(even, odd, order, rows):
    columns = even.shape[1]
    blocks = even.shape[0] // rows // 2
    kept, *sent = small_call(
        first_sum,
        [((blocks * rows, columns), jnp.float32)] + sent_shapes(blocks, rows, columns),
        even,
        exchange(odd, 1),
    )
    for distance in order[:-1]:
        onward = exchange(sent[1], distance)
        staying = exchange(sent[0], distance)
        blocks //= 2
        sent = small_call(sum_on, sent_shapes(blocks, rows, columns), kept, onward)
        [kept] = small_call(sum_kept, [((blocks * rows, columns), jnp.float32)], kept, staying)
    return kept, exchange(sent[0], order[-1])


def on_device(
    prompt_states,
    norm_gain,
    query_weight,
    key_weight,
    value_weight,
    out_weight,
    cache_keys,
    cache_values,
    block_lists,
):
    sections = lax.axis_size("section")
    heads = lax.axis_size("head")
    section_index = lax.axis_index("section")
    head_index = lax.axis_index("head")
    rows, width = prompt_states.shape[1:]
    half = width // HALVES
    tokens = rows * heads
    prefix = cache_keys.shape[1]
    group_bits = (HD // key_weight.shape[2]).bit_length() - 1
    key_weight = join_columns(key_weight, group_bits, head_index)
    value_weight = join_columns(value_weight, group_bits, head_index)
    cache = (
        join_columns(cache_keys, group_bits, head_index),
        join_columns(cache_values, group_bits, head_index),
    )

    whole_tiles = rows % 16 == 0
    block_of = jnp.arange(heads, dtype=jnp.int32) ^ head_index
    positions = (
        prefix + block_of[:, None] * rows + jnp.arange(rows, dtype=jnp.int32)[None, :]
    ).reshape(tokens)
    inverse_freq = jnp.exp(-math.log(THETA) * jnp.arange(HD // 2, dtype=jnp.float32) * 2.0 / HD)
    angles = positions.astype(jnp.float32)[:, None] * inverse_freq[None, :]
    cosine, sine = jnp.cos(angles), jnp.sin(angles)
    tables = (
        norm_gain,
        jnp.concatenate([cosine, cosine], 1),
        jnp.concatenate([-sine, sine], 1),
    )
    place = jnp.stack([section_index, head_index]).astype(jnp.int32)
    projections = (query_weight, key_weight, value_weight)
    states = [prompt_states[0, :, i * half : (i + 1) * half] for i in range(HALVES)]
    states, place, tables, projections, out_weight = lax.optimization_barrier(
        (states, place, tables, projections, out_weight)
    )

    orders = (chip_bits(), chip_bits()[::-1])
    if whole_tiles:
        targets = []
        for i, order in enumerate(orders):
            spots = {}
            for row, j in enumerate(scatter_order(order, heads)):
                spots |= {j: (2 * i, row * rows), j + 1: (2 * i + 1, row * rows)}
            targets.append(tuple(spots[j] for j in range(heads)))
        out_rows = [tokens // 2] * 2 * HALVES
    else:
        targets = [((i, 0),) for i in range(HALVES)]
        out_rows = [tokens] * HALVES

    loads = [load(projections, ((1, CHUNKS, 0, CHUNKS), (1, 1, 0, 1), (1, 1, 0, 1)))]
    output = weights = None
    for step in range(sections):
        if step:
            states = [forward(s, step) for s in states]
        if step:
            pieces = gather(states, orders)
        else:
            pieces, loaded = first_gather(prompt_states[0], loads)
            weights = [*loaded, out_weight]
        if not whole_tiles:
            pieces = [[jnp.concatenate(p, 0)] for p in pieces]
        partials = layer(
            step, sum(pieces, []), targets, out_rows, rows, weights, cache, block_lists, place, tables
        )
        made = len(out_rows)
        if not step:
            weights = [*weights[:-1], *partials[made:]]
        partials = partials[:made]
        if not whole_tiles:
            blocks = [jnp.split(p, heads, 0) for p in partials]
            partials = [
                jnp.concatenate([b[j + odd] for j in scatter_order(order, heads)], 0)
                for b, order in zip(blocks, orders)
                for odd in range(2)
            ]
        sums = [
            scatter_half(partials[2 * i], partials[2 * i + 1], order, rows)
            for i, order in enumerate(orders)
        ]
        kept, others = zip(*sums)
        states = small_call(
            last_sum, [((rows, half), jnp.bfloat16)] * HALVES, *states, *kept, *others
        )
        if step and step == sections - 1:
            place, states = lax.optimization_barrier((place, states))
            output = jnp.where(place[0] == step, jnp.concatenate(states, 1), output)
            break
        [output] = small_call(
            named(keep_output, HALVES, step),
            [((rows, width), jnp.bfloat16)],
            place,
            *states,
            *([output] if step else []),
        )
    return output[None, None]


def solution(mesh):
    return jax.shard_map(
        on_device,
        mesh=mesh,
        in_specs=(
            P(None, "head", None),
            P("section", None),
            P("section", None, "head"),
            P("section", None, "head"),
            P("section", None, "head"),
            P("section", "head", None),
            P("section", None, "head"),
            P("section", None, "head"),
            P(),
        ),
        out_specs=P("section", None, "head", None),
        check_vma=False,
    )
```
